1024 devices in a mesh: inp: 16 (over z), out: 8 (over y_hi, core), dep: 8 (over y_lo, x).
Axes of the slice: x: 4, y: 8 (y_hi: 4, y_lo: 2; y = y_hi * 2 + y_lo), z: 16, core: 2. Of those that a mesh axis runs over, the one named last changes fastest.
Arguments:
- tokens: bfloat16 [1536, 8192], P('dep', 'inp'), may hold values from -6 to 6
- grad_hidden: bfloat16 [1536, 14336], P('dep', 'out'), may hold values from -3 to 3
- w_gate: bfloat16 [8192, 14336], P('inp', 'out'), may hold values from -0.0625 to 0.0625
- w_up: bfloat16 [8192, 14336], P('inp', 'out'), may hold values from -0.0625 to 0.0625
Outputs:
- grad_input: bfloat16 [1536, 8192], P('dep', ('inp', 'out'))
- gate_grad: bfloat16 [8192, 14336], P(('inp', 'dep'), 'out')
- up_grad: bfloat16 [8192, 14336], P(('inp', 'dep'), 'out')
The draws below stay inside these ranges and needn't reach their ends.
All inputs are finite; a program needn't handle non-finite values.
Results may differ from the reference program's by a relative error of at most 0.019.
Values may be sent and summed in bfloat16 or wider, within the bound.
No kernel may reach another device: no remote copies, remote signals or barrier semaphores. Data moves between devices by JAX's collectives and lax.ppermute only.
A program may use at most 32 MiB of HBM per device.

```python
import math
import jax
import jax.numpy as jnp
from jax import lax

D = 8192
FF = 14336
TOK_DEP = 192
TOKENS = 1536
N_DEP = 8


def with_spikes(array, stream_key, source, target, parts, factor):
    def block_of(axis_at):
        return (jnp.arange(array.shape[axis_at]) // (array.shape[axis_at] // parts)).reshape((-1,) + (1,) * (array.ndim - 1 - axis_at))

    first = jax.random.permutation(stream_key, parts)[block_of(target)]
    far = (block_of(target) + parts // 2) % parts
    return jnp.where((block_of(source) == first) | (block_of(source) == far), factor * array, array)


def block_scale(key, shape, split, low, top_value):
    def one(axis_at, blocks):
        steps = jax.random.uniform(jax.random.fold_in(jax.random.fold_in(key, 6), axis_at), (blocks,), jnp.float32, low / len(split), top_value / len(split))
        return jnp.repeat(jnp.exp(steps), shape[axis_at] // blocks).reshape((-1,) + (1,) * (len(shape) - axis_at - 1))

    level = one(*split[0])
    for cut in split[1:]:
        level = level * one(*cut)
    return level


def gaussian(own_key, dims, scale, bound, cuts=(), dtype=jnp.bfloat16):
    gain = block_scale(own_key, dims, cuts, -0.22, 0.18) if cuts else 1.0
    values = jax.random.normal(own_key, dims, jnp.float32) * scale * gain
    return jnp.minimum(jnp.maximum(values, -bound), bound).astype(dtype)


def bell_draw_with(rng, extent, spread, limit, split, heavy, dtype=jnp.bfloat16):
    values = spread * jax.random.normal(rng, extent, jnp.float32)
    if split:
        values = values * block_scale(rng, extent, split, -0.22, 0.18)
    return jnp.clip(with_spikes(values, jax.random.fold_in(rng, 3), *heavy), -limit, limit).astype(dtype)


def setup_inputs(seed: int = 0) -> dict:
    seeds = jax.random.split(jax.random.key(seed), 5)
    tokens = bell_draw_with(seeds[0], (TOKENS, D), 1.0, 6.0, ((0, 8), (1, 16)), (0, 1, 16, 2.0))
    grad_hidden = gaussian(seeds[1], (TOKENS, FF), 0.5, 3.0, ((0, 8), (1, 8)))
    w_gate = gaussian(seeds[2], (D, FF), D ** -0.5, 0.0625, ((0, 16), (1, 8)))
    w_up = gaussian(seeds[3], (D, FF), D ** -0.5, 0.0625, ((0, 16), (1, 8)))
    return {"tokens": tokens, "grad_hidden": grad_hidden, "w_gate": w_gate, "w_up": w_up}


def contract_rows(left, right):
    return lax.dot_general(left, right, (((0,), (0,)), ((), ())), preferred_element_type=jnp.float32)

def contract_cols(left, right):
    return lax.dot_general(left, right, (((1,), (1,)), ((), ())), preferred_element_type=jnp.float32)

def reference(tokens, grad_hidden, w_gate, w_up):
    gate_value = jnp.dot(tokens, w_gate, preferred_element_type=jnp.float32)
    up_value = jnp.dot(tokens, w_up, preferred_element_type=jnp.float32)
    sigmoid_gate = jax.nn.sigmoid(gate_value)
    cotangent = grad_hidden.astype(jnp.float32)
    grad_gate = (cotangent * up_value * sigmoid_gate * (1.0 + gate_value * (1.0 - sigmoid_gate))).astype(jnp.bfloat16)
    grad_up = (cotangent * gate_value * sigmoid_gate).astype(jnp.bfloat16)
    grad_input = (contract_cols(grad_gate, w_gate) + contract_cols(grad_up, w_up)).astype(jnp.bfloat16)
    gate_total = jnp.zeros((D, FF), jnp.float32)
    up_total = jnp.zeros((D, FF), jnp.float32)
    for block_index in range(N_DEP):
        first_row = block_index * TOK_DEP
        token_block = tokens[first_row:first_row + TOK_DEP]
        gate_part = contract_rows(token_block, grad_gate[first_row:first_row + TOK_DEP]).astype(jnp.bfloat16)
        up_part = contract_rows(token_block, grad_up[first_row:first_row + TOK_DEP]).astype(jnp.bfloat16)
        gate_part = lax.optimization_barrier(gate_part)
        up_part = lax.optimization_barrier(up_part)
        gate_total = gate_total + gate_part.astype(jnp.float32)
        up_total = up_total + up_part.astype(jnp.float32)
    factor = 1.0 / math.sqrt(TOKENS)
    return (grad_input, (gate_total * factor).astype(jnp.bfloat16), (up_total * factor).astype(jnp.bfloat16))
```

```python
import math

import jax
import jax.numpy as jnp
from jax import lax
from jax.sharding import PartitionSpec as P

BF16 = jnp.bfloat16
F32 = jnp.float32
LANES = 128


def product(left, right):
    return jnp.dot(left, right, preferred_element_type=F32)


def contract_rows(left, right):
    return lax.dot_general(left, right, (((0,), (0,)), ((), ())), preferred_element_type=F32)


def contract_cols(left, right):
    return lax.dot_general(left, right, (((1,), (1,)), ((), ())), preferred_element_type=F32)


def shards(tokens, grad_hidden, w_gate, w_up):
    token_count, feature_count = tokens.shape
    hidden = w_gate.shape[1]
    inp, out, dep = (lax.axis_size(name) for name in ("inp", "out", "dep"))
    factor = 1.0 / math.sqrt(token_count * dep)
    half = hidden // 2
    group = inp // 2
    rows = token_count // group
    pairs = [(i, i ^ 1) for i in range(inp)]
    alike = [[p + 2 * i for i in range(group)] for p in range(2)]
    place = lax.axis_index("inp")
    parity = place % 2
    even = parity == 0

    all_tokens = lax.all_to_all(
        jnp.broadcast_to(tokens[None], (dep, token_count, feature_count)), "dep", 0, 0
    ).reshape(dep * token_count, feature_count)

    halves = [
        jnp.concatenate(
            [
                product(tokens, w_gate[:, h * half : (h + 1) * half]),
                product(tokens, w_up[:, h * half : (h + 1) * half]),
            ],
            axis=1,
        )
        for h in range(2)
    ]
    given = jnp.where(even, halves[1], halves[0]).astype(BF16)
    kept = jnp.where(even, halves[0], halves[1])
    kept = (kept + lax.ppermute(given, "inp", pairs).astype(F32)).astype(BF16)
    terms = lax.all_to_all(
        kept.reshape(group, rows, hidden), "inp", 0, 0, axis_index_groups=alike
    )
    summed = jnp.sum(terms.astype(F32), axis=0)
    gate_value = summed[:, :half]
    up_value = summed[:, half:]
    cotangent = lax.dynamic_slice(
        grad_hidden, ((place // 2) * rows, parity * half), (rows, half)
    ).astype(F32)
    sigmoid_gate = jax.nn.sigmoid(gate_value)
    grad_gate = cotangent * up_value * sigmoid_gate * (1.0 + gate_value * (1.0 - sigmoid_gate))
    grad_upper = cotangent * gate_value * sigmoid_gate
    paired = jnp.concatenate([grad_gate, grad_upper], axis=1).astype(BF16)
    own = lax.all_gather(paired, "inp", axis=0, tiled=True, axis_index_groups=alike)
    other = lax.ppermute(own, "inp", pairs)

    width = 2 * LANES
    blocks = dep // 2
    starts = [min(b * width, half - width) for b in range(blocks)]
    skips = [b * width - s for b, s in enumerate(starts)]

    def weight_gradient(pair):
        pieces = jnp.stack(
            [pair[:, u * half + s : u * half + s + width] for u in range(2) for s in starts]
        )
        block = lax.all_to_all(pieces, "dep", 0, 0).reshape(dep * token_count, width)
        grad = (contract_rows(all_tokens, block) * factor).astype(BF16)
        swapped = lax.all_to_all(grad.reshape(dep, feature_count // dep, width), "dep", 0, 0)
        return [
            jnp.concatenate(
                [swapped[u * blocks + b][:, skips[b] :] for b in range(blocks)], axis=1
            )
            for u in range(2)
        ]

    own_grads = weight_gradient(own)
    other_grads = weight_gradient(other)
    gate_grad, up_grad = (
        jnp.concatenate([jnp.where(even, a, b), jnp.where(even, b, a)], axis=1)
        for a, b in zip(own_grads, other_grads)
    )

    full = [jnp.where(even, own, other), jnp.where(even, other, own)]
    input_terms = sum(
        contract_cols(w[:, h * half : (h + 1) * half], full[h][:, u * half : (u + 1) * half])
        for h in range(2)
        for u, w in enumerate((w_gate, w_up))
    ).astype(BF16)
    shares = lax.all_to_all(
        input_terms.reshape(out, feature_count // out, token_count), "out", 0, 0
    )
    grad_input = jnp.sum(shares.astype(F32), axis=0).astype(BF16).T
    return grad_input, gate_grad, up_grad


def solution(mesh):
    return jax.shard_map(
        shards,
        mesh=mesh,
        in_specs=(P("dep", "inp"), P("dep", "out"), P("inp", "out"), P("inp", "out")),
        out_specs=(P("dep", ("inp", "out")), P(("inp", "dep"), "out"), P(("inp", "dep"), "out")),
        check_vma=False,
    )
```

```python
import math

import jax
import jax.numpy as jnp
from jax import lax
from jax.sharding import PartitionSpec as P

BF16 = jnp.bfloat16
F32 = jnp.float32
LANES = 128


def product(left, right):
    return jnp.dot(left, right, preferred_element_type=F32)


def contract_rows(left, right):
    return lax.dot_general(left, right, (((0,), (0,)), ((), ())), preferred_element_type=F32)


def contract_cols(left, right):
    return lax.dot_general(left, right, (((1,), (1,)), ((), ())), preferred_element_type=F32)


def shards(tokens, grad_hidden, w_gate, w_up):
    token_count, feature_count = tokens.shape
    hidden = w_gate.shape[1]
    inp, out, dep = (lax.axis_size(name) for name in ("inp", "out", "dep"))
    factor = 1.0 / math.sqrt(token_count * dep)
    half = hidden // 2
    group = inp // 2
    rows = token_count // group
    pairs = [(i, i ^ 1) for i in range(inp)]
    alike = [[p + 2 * i for i in range(group)] for p in range(2)]
    place = lax.axis_index("inp")
    parity = place % 2
    even = parity == 0

    all_tokens = lax.all_gather(tokens, "dep", axis=0, tiled=True)

    halves = [
        jnp.concatenate(
            [
                product(tokens, w_gate[:, h * half : (h + 1) * half]),
                product(tokens, w_up[:, h * half : (h + 1) * half]),
            ],
            axis=1,
        )
        for h in range(2)
    ]
    given = jnp.where(even, halves[1], halves[0]).astype(BF16)
    kept = jnp.where(even, halves[0], halves[1])
    kept = (kept + lax.ppermute(given, "inp", pairs).astype(F32)).astype(BF16)
    terms = lax.all_to_all(
        kept.reshape(group, rows, hidden), "inp", 0, 0, axis_index_groups=alike
    )
    summed = jnp.sum(terms.astype(F32), axis=0)
    gate_value = summed[:, :half]
    up_value = summed[:, half:]
    cotangent = lax.dynamic_slice(
        grad_hidden, ((place // 2) * rows, parity * half), (rows, half)
    ).astype(F32)
    sigmoid_gate = jax.nn.sigmoid(gate_value)
    grad_gate = cotangent * up_value * sigmoid_gate * (1.0 + gate_value * (1.0 - sigmoid_gate))
    grad_upper = cotangent * gate_value * sigmoid_gate
    paired = jnp.concatenate([grad_gate, grad_upper], axis=1).astype(BF16)
    own = lax.all_gather(paired, "inp", axis=0, tiled=True, axis_index_groups=alike)
    other = lax.ppermute(own, "inp", pairs)

    width = 2 * LANES
    blocks = dep // 2
    starts = [min(b * width, half - width) for b in range(blocks)]
    skips = [b * width - s for b, s in enumerate(starts)]

    def column_block(pair):
        pieces = jnp.stack(
            [pair[:, u * half + s : u * half + s + width] for u in range(2) for s in starts]
        )
        return lax.all_to_all(pieces, "dep", 0, 0).reshape(dep * token_count, width)

    own_block = column_block(own)
    other_block = column_block(other)

    first = [jnp.where(even, own, other), jnp.where(even, other, own)]
    terms = sum(
        contract_cols(w[:, h * half : (h + 1) * half], first[h][:, u * half : (u + 1) * half])
        for h in range(2)
        for u, w in enumerate((w_gate, w_up))
    )
    at_out = lax.axis_index("out")
    terms = terms.reshape(out // 2, 2, feature_count // out, token_count)
    low = at_out % 2 == 0
    given = jnp.where(low, terms[:, 1], terms[:, 0]).astype(BF16)
    kept = jnp.where(low, terms[:, 0], terms[:, 1])
    kept = kept + lax.ppermute(given, "out", [(i, i ^ 1) for i in range(out)]).astype(F32)
    bit = out // 2
    while bit > 1:
        low = at_out & bit == 0
        middle = kept.shape[0] // 2
        given = jnp.where(low, kept[middle:], kept[:middle]).astype(BF16)
        kept = jnp.where(low, kept[:middle], kept[middle:])
        swaps = [(i, i ^ bit) for i in range(out)]
        kept = kept + lax.ppermute(given, "out", swaps).astype(F32)
        bit //= 2
    grad_input = kept[0].astype(BF16).T

    grad = contract_rows(all_tokens, jnp.concatenate([own_block, other_block], axis=1))
    grad = (grad * factor).astype(BF16)
    swapped = lax.all_to_all(grad.reshape(dep, feature_count // dep, 2 * width), "dep", 0, 0)

    def columns(u, side):
        return [
            swapped[u * blocks + b][:, side * width + skips[b] : (side + 1) * width]
            for b in range(blocks)
        ]

    def assembled(u):
        own_part = jnp.concatenate(columns(u, 0), axis=1)
        other_part = jnp.concatenate(columns(u, 1), axis=1)
        return jnp.concatenate(
            [jnp.where(even, own_part, other_part), jnp.where(even, other_part, own_part)], axis=1
        )

    return grad_input, assembled(0), assembled(1)


def solution(mesh):
    return jax.shard_map(
        shards,
        mesh=mesh,
        in_specs=(P("dep", "inp"), P("dep", "out"), P("inp", "out"), P("inp", "out")),
        out_specs=(P("dep", ("inp", "out")), P(("inp", "dep"), "out"), P(("inp", "dep"), "out")),
        check_vma=False,
    )
```

```python
import functools
import math

import jax
import jax.numpy as jnp
from jax import lax
from jax.experimental import pallas as pl
from jax.experimental.pallas import tpu as pltpu
from jax.sharding import PartitionSpec as P

BF16 = jnp.bfloat16
F32 = jnp.float32
LANES = 128
ROWS_BY_COLS = (((1,), (0,)), ((), ()))
COLS_BY_COLS = (((1,), (1,)), ((), ()))


def values_kernel(side_ref, tokens_ref, gate_ref, up_ref, out_ref):
    del side_ref
    half = gate_ref.shape[1]
    tokens = tokens_ref[...]
    for u, w_ref in enumerate((gate_ref, up_ref)):
        part = lax.dot_general(tokens, w_ref[...], ROWS_BY_COLS, preferred_element_type=F32)
        out_ref[:, u * half : (u + 1) * half] = part.astype(out_ref.dtype)


def partial_values(side, tokens, w_gate, w_up, dtype):
    token_count, feature_count = tokens.shape
    half = w_gate.shape[1] // 2
    weights = pl.BlockSpec((feature_count, half), lambda g, s: (0, s[0]))
    return pl.pallas_call(
        values_kernel,
        out_shape=jax.ShapeDtypeStruct((token_count, 2 * half), dtype),
        grid_spec=pltpu.PrefetchScalarGridSpec(
            num_scalar_prefetch=1,
            grid=(1,),
            in_specs=[
                pl.BlockSpec((token_count, feature_count), lambda g, s: (0, 0)),
                weights,
                weights,
            ],
            out_specs=pl.BlockSpec((token_count, 2 * half), lambda g, s: (0, 0)),
        ),
        compiler_params=pltpu.CompilerParams(vmem_limit_bytes=24 * 2**20),
        cost_estimate=pl.CostEstimate(
            flops=4 * token_count * feature_count * half,
            bytes_accessed=4 * feature_count * half + 8 * token_count * half,
            transcendentals=0,
        ),
    )(side, tokens, w_gate, w_up)


def grads_kernel(starts, terms_ref, cotangent_ref, pieces_ref):
    half = cotangent_ref.shape[1]
    width = pieces_ref.shape[2]
    values = terms_ref[0].astype(F32)
    for k in range(1, terms_ref.shape[0]):
        values = values + terms_ref[k].astype(F32)
    gate_value = values[:, :half]
    up_value = values[:, half:]
    cotangent = cotangent_ref[...].astype(F32)
    sigmoid_gate = jax.nn.sigmoid(gate_value)
    grad_gate = cotangent * up_value * sigmoid_gate * (1.0 + gate_value * (1.0 - sigmoid_gate))
    grad_upper = cotangent * gate_value * sigmoid_gate
    for u, grad in enumerate((grad_gate, grad_upper)):
        grad = grad.astype(BF16)
        for b, start in enumerate(starts):
            pieces_ref[u * len(starts) + b] = grad[:, start : start + width]


def grad_pieces(terms, cotangent, starts, width):
    rows, half = cotangent.shape
    return pl.pallas_call(
        functools.partial(grads_kernel, starts),
        out_shape=jax.ShapeDtypeStruct((2 * len(starts), rows, width), BF16),
        compiler_params=pltpu.CompilerParams(vmem_limit_bytes=16 * 2**20),
        cost_estimate=pl.CostEstimate(
            flops=40 * rows * half,
            bytes_accessed=2 * terms.size + 8 * rows * half,
            transcendentals=rows * half,
        ),
    )(terms, cotangent)


def input_kernel(starts, skips, side_ref, gate_ref, up_ref, pieces_ref, *rest):
    total_ref, out_ref = rest if len(rest) == 2 else (None, rest[0])
    del side_ref
    width = pieces_ref.shape[2]
    total = None if total_ref is None else total_ref[...]
    for u, w_ref in enumerate((gate_ref, up_ref)):
        for b, (start, skip) in enumerate(zip(starts, skips)):
            term = lax.dot_general(
                w_ref[:, start + skip : start + width],
                pieces_ref[u * len(starts) + b][:, skip:],
                COLS_BY_COLS,
                preferred_element_type=F32,
            )
            total = term if total is None else total + term
    out_ref[...] = total


def input_terms(side, w_gate, w_up, pieces, starts, skips, total=None):
    feature_count = w_gate.shape[0]
    half = w_gate.shape[1] // 2
    token_count = pieces.shape[1]
    weights = pl.BlockSpec((feature_count, half), lambda g, s: (0, s[0]))
    result = pl.BlockSpec((feature_count, token_count), lambda g, s: (0, 0))
    more = () if total is None else (total,)
    return pl.pallas_call(
        functools.partial(input_kernel, starts, skips),
        out_shape=jax.ShapeDtypeStruct((feature_count, token_count), F32),
        grid_spec=pltpu.PrefetchScalarGridSpec(
            num_scalar_prefetch=1,
            grid=(1,),
            in_specs=[weights, weights, pl.BlockSpec(pieces.shape, lambda g, s: (0, 0, 0))]
            + [result] * len(more),
            out_specs=result,
        ),
        compiler_params=pltpu.CompilerParams(vmem_limit_bytes=24 * 2**20),
        cost_estimate=pl.CostEstimate(
            flops=4 * token_count * feature_count * half,
            bytes_accessed=4 * feature_count * half + 8 * token_count * half,
            transcendentals=0,
        ),
    )(side, w_gate, w_up, pieces, *more)


def weight_kernel(factor, tokens_ref, own_ref, other_ref, out_ref):
    dep = tokens_ref.shape[0]
    width = own_ref.shape[2]
    for side, block_ref in enumerate((own_ref, other_ref)):
        total = None
        for d in range(dep):
            term = lax.dot_general(
                tokens_ref[d], block_ref[d], ROWS_BY_COLS, preferred_element_type=F32
            )
            total = term if total is None else total + term
        out_ref[:, side * width : (side + 1) * width] = (total * factor).astype(BF16)


def weight_terms(tokens, own, other, factor):
    dep, feature_count, token_count = tokens.shape
    width = own.shape[2]
    return pl.pallas_call(
        functools.partial(weight_kernel, factor),
        out_shape=jax.ShapeDtypeStruct((feature_count, 2 * width), BF16),
        compiler_params=pltpu.CompilerParams(vmem_limit_bytes=24 * 2**20),
        cost_estimate=pl.CostEstimate(
            flops=4 * dep * token_count * feature_count * width,
            bytes_accessed=2 * dep * token_count * (feature_count + 2 * width),
            transcendentals=0,
        ),
    )(tokens, own, other)


def shards(tokens, grad_hidden, w_gate, w_up):
    token_count, feature_count = tokens.shape
    hidden = w_gate.shape[1]
    inp, out, dep = (lax.axis_size(name) for name in ("inp", "out", "dep"))
    factor = 1.0 / math.sqrt(token_count * dep)
    half = hidden // 2
    group = inp // 2
    rows = token_count // group
    pairs = [(i, i ^ 1) for i in range(inp)]
    alike = [[p + 2 * i for i in range(group)] for p in range(2)]
    place = lax.axis_index("inp")
    parity = place % 2
    even = parity == 0
    own_side = parity.reshape(1)
    other_side = 1 - own_side

    given = partial_values(other_side, tokens, w_gate, w_up, BF16)
    kept = partial_values(own_side, tokens, w_gate, w_up, F32)
    kept = (kept + lax.ppermute(given, "inp", pairs).astype(F32)).astype(BF16)

    all_tokens = lax.all_gather(tokens.T, "dep", axis=0)

    terms = lax.all_to_all(
        kept.reshape(group, rows, hidden), "inp", 0, 0, axis_index_groups=alike
    )
    cotangent = lax.dynamic_slice(
        grad_hidden, ((place // 2) * rows, parity * half), (rows, half)
    )

    width = 2 * LANES
    blocks = dep // 2
    starts = [min(b * width, half - width) for b in range(blocks)]
    skips = [b * width - s for b, s in enumerate(starts)]
    pieces = grad_pieces(terms, cotangent, starts, width)
    own = lax.all_gather(pieces, "inp", axis=1, tiled=True, axis_index_groups=alike)
    other = lax.ppermute(own, "inp", pairs)

    shares = input_terms(own_side, w_gate, w_up, own, starts, skips)
    own, shares = lax.optimization_barrier((own, shares))
    own_block = lax.all_to_all(own, "dep", 0, 0)
    shares = input_terms(other_side, w_gate, w_up, other, starts, skips, shares)
    other, shares, all_tokens = lax.optimization_barrier((other, shares, all_tokens))
    other_block = lax.all_to_all(other, "dep", 0, 0)
    at_out = lax.axis_index("out")
    shares = shares.reshape(out // 2, 2, feature_count // out, token_count)
    low = at_out % 2 == 0
    given = jnp.where(low, shares[:, 1], shares[:, 0]).astype(BF16)
    kept = jnp.where(low, shares[:, 0], shares[:, 1])
    kept = kept + lax.ppermute(given, "out", [(i, i ^ 1) for i in range(out)]).astype(F32)
    bit = out // 2
    while bit > 1:
        low = at_out & bit == 0
        middle = kept.shape[0] // 2
        given = jnp.where(low, kept[middle:], kept[:middle]).astype(BF16)
        kept = jnp.where(low, kept[:middle], kept[middle:])
        swaps = [(i, i ^ bit) for i in range(out)]
        kept = kept + lax.ppermute(given, "out", swaps).astype(F32)
        if bit == out // 2:
            own_block, kept = lax.optimization_barrier((own_block, kept))
        bit //= 2
    grad_input = kept[0].astype(BF16).T

    grad = weight_terms(all_tokens, own_block, other_block, factor)
    swapped = lax.all_to_all(grad.reshape(dep, feature_count // dep, 2 * width), "dep", 0, 0)

    def columns(u, side):
        return [
            swapped[u * blocks + b][:, side * width + skips[b] : (side + 1) * width]
            for b in range(blocks)
        ]

    def assembled(u):
        own_part = jnp.concatenate(columns(u, 0), axis=1)
        other_part = jnp.concatenate(columns(u, 1), axis=1)
        return jnp.concatenate(
            [jnp.where(even, own_part, other_part), jnp.where(even, other_part, own_part)], axis=1
        )

    return grad_input, assembled(0), assembled(1)


def solution(mesh):
    return jax.shard_map(
        shards,
        mesh=mesh,
        in_specs=(P("dep", "inp"), P("dep", "out"), P("inp", "out"), P("inp", "out")),
        out_specs=(P("dep", ("inp", "out")), P(("inp", "dep"), "out"), P(("inp", "dep"), "out")),
        check_vma=False,
    )
```

```python
import functools
import math

import jax
import jax.numpy as jnp
from jax import lax
from jax.experimental import pallas as pl
from jax.experimental.pallas import tpu as pltpu
from jax.sharding import PartitionSpec as P

BF16 = jnp.bfloat16
F32 = jnp.float32
LANES = 128
CHUNKS = 2
ROWS_BY_COLS = (((1,), (0,)), ((), ()))
COLS_BY_COLS = (((1,), (1,)), ((), ()))


def fetch_half(side, hbm_refs, vmem_refs, sems):
    copies = []
    for w, (src, dst) in enumerate(zip(hbm_refs, vmem_refs)):
        half = dst.shape[1]
        rows = dst.shape[0] // CHUNKS
        first = pl.multiple_of(side * half, LANES)
        for c in range(CHUNKS):
            copy = pltpu.make_async_copy(
                src.at[pl.ds(c * rows, rows), pl.ds(first, half)],
                dst.at[pl.ds(c * rows, rows), :],
                sems.at[w, c],
            )
            copy.start()
            copies.append(copy)
    return copies


def values_kernel(side_ref, tokens_ref, gate_hbm, up_hbm, out_ref, gate_ref, up_ref, sems):
    copies = fetch_half(side_ref[0], (gate_hbm, up_hbm), (gate_ref, up_ref), sems)
    half = gate_ref.shape[1]
    for u, w_ref in enumerate((gate_ref, up_ref)):
        for copy in copies[u * CHUNKS : (u + 1) * CHUNKS]:
            copy.wait()
        part = lax.dot_general(
            tokens_ref[...], w_ref[...], ROWS_BY_COLS, preferred_element_type=F32
        )
        out_ref[:, u * half : (u + 1) * half] = part.astype(out_ref.dtype)


def half_scratch(w_gate):
    half = pltpu.VMEM((w_gate.shape[0], w_gate.shape[1] // 2), BF16)
    return [half, half, pltpu.SemaphoreType.DMA((2, CHUNKS))]


IN_HBM = pl.BlockSpec(memory_space=pltpu.HBM)
IN_SMEM = pl.BlockSpec(memory_space=pltpu.SMEM)
IN_VMEM = pl.BlockSpec(memory_space=pltpu.VMEM)
PARAMS = pltpu.CompilerParams(vmem_limit_bytes=16 * 2**20)
WHOLE = pltpu.CompilerParams(vmem_limit_bytes=60 * 2**20)


def partial_values(side, tokens, w_gate, w_up, dtype):
    token_count, feature_count = tokens.shape
    half = w_gate.shape[1] // 2
    return pl.pallas_call(
        values_kernel,
        out_shape=jax.ShapeDtypeStruct((token_count, 2 * half), dtype),
        in_specs=[IN_SMEM, IN_VMEM, IN_HBM, IN_HBM],
        out_specs=IN_VMEM,
        scratch_shapes=half_scratch(w_gate),
        compiler_params=WHOLE,
        cost_estimate=pl.CostEstimate(
            flops=4 * token_count * feature_count * half,
            bytes_accessed=4 * feature_count * half + 8 * token_count * half,
            transcendentals=0,
        ),
    )(side, tokens, w_gate, w_up)


def grads_kernel(terms_ref, cotangent_ref, pair_ref):
    half = cotangent_ref.shape[1]
    values = terms_ref[0].astype(F32)
    for k in range(1, terms_ref.shape[0]):
        values = values + terms_ref[k].astype(F32)
    gate_value = values[:, :half]
    up_value = values[:, half:]
    cotangent = cotangent_ref[...].astype(F32)
    sigmoid_gate = jax.nn.sigmoid(gate_value)
    grad_gate = cotangent * up_value * sigmoid_gate * (1.0 + gate_value * (1.0 - sigmoid_gate))
    grad_upper = cotangent * gate_value * sigmoid_gate
    pair_ref[:, :half] = grad_gate.astype(BF16)
    pair_ref[:, half:] = grad_upper.astype(BF16)


def grad_pair(terms, cotangent):
    rows, half = cotangent.shape
    return pl.pallas_call(
        grads_kernel,
        out_shape=jax.ShapeDtypeStruct((rows, 2 * half), BF16),
        compiler_params=PARAMS,
        cost_estimate=pl.CostEstimate(
            flops=40 * rows * half,
            bytes_accessed=2 * terms.size + 8 * rows * half,
            transcendentals=rows * half,
        ),
    )(terms, cotangent)


def pieces_kernel(starts, pair_ref, pieces_ref):
    half = pair_ref.shape[1] // 2
    width = pieces_ref.shape[2]
    for u in range(2):
        for b, start in enumerate(starts):
            first = u * half + start
            pieces_ref[u * len(starts) + b] = pair_ref[:, first : first + width]


def dep_pieces(pair, starts, width):
    shape = (2 * len(starts), pair.shape[0], width)
    return pl.pallas_call(
        functools.partial(pieces_kernel, starts),
        out_shape=jax.ShapeDtypeStruct(shape, BF16),
        compiler_params=PARAMS,
        cost_estimate=pl.CostEstimate(
            flops=0, bytes_accessed=4 * math.prod(shape), transcendentals=0
        ),
    )(pair)


def input_kernel(side_ref, gate_hbm, up_hbm, pair_ref, *rest):
    *totals, out_ref, gate_ref, up_ref, sems = rest
    copies = fetch_half(side_ref[0], (gate_hbm, up_hbm), (gate_ref, up_ref), sems)
    half = gate_ref.shape[1]
    total = totals[0][...] if totals else None
    for u, w_ref in enumerate((gate_ref, up_ref)):
        for copy in copies[u * CHUNKS : (u + 1) * CHUNKS]:
            copy.wait()
        term = lax.dot_general(
            w_ref[...],
            pair_ref[:, u * half : (u + 1) * half],
            COLS_BY_COLS,
            preferred_element_type=F32,
        )
        total = term if total is None else total + term
    out_ref[...] = total.astype(out_ref.dtype)


def input_terms(side, w_gate, w_up, pair, dtype, *total):
    feature_count = w_gate.shape[0]
    half = w_gate.shape[1] // 2
    token_count = pair.shape[0]
    return pl.pallas_call(
        input_kernel,
        out_shape=jax.ShapeDtypeStruct((feature_count, token_count), dtype),
        in_specs=[IN_SMEM, IN_HBM, IN_HBM, IN_VMEM] + [IN_VMEM] * len(total),
        out_specs=IN_VMEM,
        scratch_shapes=half_scratch(w_gate),
        compiler_params=WHOLE,
        cost_estimate=pl.CostEstimate(
            flops=4 * token_count * feature_count * half,
            bytes_accessed=4 * feature_count * half + 8 * token_count * half,
            transcendentals=0,
        ),
    )(side, w_gate, w_up, pair, *total)


def weight_kernel(factor, tokens_ref, own_ref, other_ref, out_ref):
    width = own_ref.shape[1]
    for side, block_ref in enumerate((own_ref, other_ref)):
        total = lax.dot_general(
            tokens_ref[...], block_ref[...], ROWS_BY_COLS, preferred_element_type=F32
        )
        out_ref[:, side * width : (side + 1) * width] = (total * factor).astype(BF16)


def weight_terms(tokens, own, other, factor):
    feature_count, token_count = tokens.shape
    width = own.shape[1]
    return pl.pallas_call(
        functools.partial(weight_kernel, factor),
        out_shape=jax.ShapeDtypeStruct((feature_count, 2 * width), BF16),
        compiler_params=PARAMS,
        cost_estimate=pl.CostEstimate(
            flops=4 * token_count * feature_count * width,
            bytes_accessed=2 * token_count * (feature_count + 2 * width),
            transcendentals=0,
        ),
    )(tokens, own, other)


def finish_kernel(skips, side_ref, swapped_ref, gate_ref, up_ref):
    width = swapped_ref.shape[2] // 2
    half = gate_ref.shape[1] // 2
    blocks = len(skips)
    for u, out_ref in enumerate((gate_ref, up_ref)):
        for s in range(2):
            first = (side_ref[0] if s == 0 else 1 - side_ref[0]) * half
            for b, skip in enumerate(skips):
                at = pl.multiple_of(first + b * width, LANES)
                out_ref[:, pl.ds(at, width - skip)] = swapped_ref[u * blocks + b][
                    :, s * width + skip : (s + 1) * width
                ]


def finished(side, swapped, half, skips):
    shape = jax.ShapeDtypeStruct((swapped.shape[1], 2 * half), BF16)
    return pl.pallas_call(
        functools.partial(finish_kernel, skips),
        out_shape=(shape, shape),
        in_specs=[IN_SMEM, IN_VMEM],
        out_specs=(IN_VMEM, IN_VMEM),
        compiler_params=PARAMS,
        cost_estimate=pl.CostEstimate(
            flops=0, bytes_accessed=4 * swapped.size, transcendentals=0
        ),
    )(side, swapped)


def shards(tokens, grad_hidden, w_gate, w_up):
    token_count, feature_count = tokens.shape
    hidden = w_gate.shape[1]
    inp, out, dep = (lax.axis_size(name) for name in ("inp", "out", "dep"))
    factor = 1.0 / math.sqrt(token_count * dep)
    half = hidden // 2
    group = inp // 2
    rows = token_count // group
    pairs = [(i, i ^ 1) for i in range(inp)]
    alike = [[p + 2 * i for i in range(group)] for p in range(2)]
    place = lax.axis_index("inp")
    parity = place % 2
    own_side = parity.reshape(1)
    other_side = 1 - own_side

    given = partial_values(other_side, tokens, w_gate, w_up, BF16)
    kept = partial_values(own_side, tokens, w_gate, w_up, F32)
    kept = (kept + lax.ppermute(given, "inp", pairs).astype(F32)).astype(BF16)

    all_tokens = lax.all_gather(tokens, "dep", axis=0, tiled=True)

    terms = lax.all_to_all(
        kept.reshape(group, rows, hidden), "inp", 0, 0, axis_index_groups=alike
    )
    cotangent = lax.dynamic_slice(
        grad_hidden, ((place // 2) * rows, parity * half), (rows, half)
    )
    own = lax.all_gather(
        grad_pair(terms, cotangent), "inp", axis=0, tiled=True, axis_index_groups=alike
    )
    other = lax.ppermute(own, "inp", pairs)

    width = 2 * LANES
    blocks = dep // 2
    starts = [min(b * width, half - width) for b in range(blocks)]
    skips = [b * width - s for b, s in enumerate(starts)]
    own_block = lax.all_to_all(dep_pieces(own, starts, width), "dep", 0, 0)
    own_block = own_block.reshape(dep * token_count, width)
    shares = input_terms(own_side, w_gate, w_up, own, F32)
    own_block, across, shares = lax.optimization_barrier((own_block, all_tokens.T, shares))
    other_block = lax.ppermute(own_block, "inp", pairs)

    shares = input_terms(other_side, w_gate, w_up, other, BF16, shares)
    shares = lax.all_to_all(
        shares.reshape(out, feature_count // out, token_count), "out", 0, 0
    )
    grad_input = jnp.sum(shares.astype(F32), axis=0).astype(BF16).T

    grad = weight_terms(across, own_block, other_block, factor)
    swapped = lax.all_to_all(grad.reshape(dep, feature_count // dep, 2 * width), "dep", 0, 0)
    gate_grad, up_grad = finished(own_side, swapped, half, skips)
    return grad_input, gate_grad, up_grad


def solution(mesh):
    return jax.shard_map(
        shards,
        mesh=mesh,
        in_specs=(P("dep", "inp"), P("dep", "out"), P("inp", "out"), P("inp", "out")),
        out_specs=(P("dep", ("inp", "out")), P(("inp", "dep"), "out"), P(("inp", "dep"), "out")),
        check_vma=False,
    )
```

```python
import functools
import math

import jax
import jax.numpy as jnp
from jax import lax
from jax.experimental import pallas as pl
from jax.experimental.pallas import tpu as pltpu
from jax.sharding import PartitionSpec as P

BF16 = jnp.bfloat16
F32 = jnp.float32
LANES = 128
ROWS_BY_COLS = (((1,), (0,)), ((), ()))
COLS_BY_COLS = (((1,), (1,)), ((), ()))


def values_kernel(
    side_ref, tokens_hbm, gate_hbm, up_hbm, out_hbm, tokens_ref, gate_ref, up_ref, out_ref, sems
):
    half = gate_ref.shape[1]
    columns = pl.ds(pl.multiple_of(side_ref[0] * half, LANES), half)
    fetches = [
        pltpu.make_async_copy(tokens_hbm, tokens_ref, sems.at[0]),
        pltpu.make_async_copy(gate_hbm.at[:, columns], gate_ref, sems.at[1]),
        pltpu.make_async_copy(up_hbm.at[:, columns], up_ref, sems.at[2]),
    ]
    for fetch in fetches:
        fetch.start()
    fetches[0].wait()
    stores = []
    for u, w_ref in enumerate((gate_ref, up_ref)):
        fetches[1 + u].wait()
        part = lax.dot_general(
            tokens_ref[...], w_ref[...], ROWS_BY_COLS, preferred_element_type=F32
        )
        out_ref[u] = part.astype(out_ref.dtype)
        store = pltpu.make_async_copy(
            out_ref.at[u], out_hbm.at[:, pl.ds(u * half, half)], sems.at[3 + u]
        )
        store.start()
        stores.append(store)
    for store in stores:
        store.wait()


IN_HBM = pl.BlockSpec(memory_space=pltpu.HBM)
IN_SMEM = pl.BlockSpec(memory_space=pltpu.SMEM)
IN_VMEM = pl.BlockSpec(memory_space=pltpu.VMEM)
PARAMS = pltpu.CompilerParams(vmem_limit_bytes=16 * 2**20)
WHOLE = pltpu.CompilerParams(vmem_limit_bytes=60 * 2**20)


def partial_values(side, tokens, w_gate, w_up):
    token_count, feature_count = tokens.shape
    half = w_gate.shape[1] // 2
    return pl.pallas_call(
        values_kernel,
        out_shape=jax.ShapeDtypeStruct((token_count, 2 * half), BF16),
        in_specs=[IN_SMEM, IN_HBM, IN_HBM, IN_HBM],
        out_specs=IN_HBM,
        scratch_shapes=[
            pltpu.VMEM((token_count, feature_count), BF16),
            pltpu.VMEM((feature_count, half), BF16),
            pltpu.VMEM((feature_count, half), BF16),
            pltpu.VMEM((2, token_count, half), BF16),
            pltpu.SemaphoreType.DMA((5,)),
        ],
        compiler_params=WHOLE,
        cost_estimate=pl.CostEstimate(
            flops=4 * token_count * feature_count * half,
            bytes_accessed=4 * feature_count * half + 4 * token_count * half,
            transcendentals=0,
        ),
    )(side, tokens, w_gate, w_up)


def grads_kernel(terms_ref, cotangent_ref, pair_ref):
    half = cotangent_ref.shape[1]
    values = terms_ref[0].astype(F32)
    for k in range(1, terms_ref.shape[0]):
        values = values + terms_ref[k].astype(F32)
    gate_value = values[:, :half]
    up_value = values[:, half:]
    cotangent = cotangent_ref[...].astype(F32)
    sigmoid_gate = jax.nn.sigmoid(gate_value)
    grad_gate = cotangent * up_value * sigmoid_gate * (1.0 + gate_value * (1.0 - sigmoid_gate))
    grad_upper = cotangent * gate_value * sigmoid_gate
    pair_ref[:, :half] = grad_gate.astype(BF16)
    pair_ref[:, half:] = grad_upper.astype(BF16)


def grad_pair(terms, cotangent):
    rows, half = cotangent.shape
    return pl.pallas_call(
        grads_kernel,
        out_shape=jax.ShapeDtypeStruct((rows, 2 * half), BF16),
        compiler_params=PARAMS,
        cost_estimate=pl.CostEstimate(
            flops=40 * rows * half,
            bytes_accessed=2 * terms.size + 8 * rows * half,
            transcendentals=rows * half,
        ),
    )(terms, cotangent)


def pieces_kernel(starts, pair_ref, pieces_ref):
    half = pair_ref.shape[1] // 2
    width = pieces_ref.shape[2]
    for u in range(2):
        for b, start in enumerate(starts):
            first = u * half + start
            pieces_ref[u * len(starts) + b] = pair_ref[:, first : first + width]


def dep_pieces(pair, starts, width):
    shape = (2 * len(starts), pair.shape[0], width)
    return pl.pallas_call(
        functools.partial(pieces_kernel, starts),
        out_shape=jax.ShapeDtypeStruct(shape, BF16),
        compiler_params=PARAMS,
        cost_estimate=pl.CostEstimate(
            flops=0, bytes_accessed=4 * math.prod(shape), transcendentals=0
        ),
    )(pair)


def own_input_kernel(gate_ref, up_ref, pair_ref, out_ref):
    half = gate_ref.shape[1]
    out_ref[...] = sum(
        lax.dot_general(
            w_ref[...],
            pair_ref[:, u * half : (u + 1) * half],
            COLS_BY_COLS,
            preferred_element_type=F32,
        )
        for u, w_ref in enumerate((gate_ref, up_ref))
    )


def other_input_kernel(core_ref, gate_ref, up_ref, pair_ref, own_ref, kept_ref, given_ref, total):
    own_input_kernel(gate_ref, up_ref, pair_ref, total)
    blocks, rows, _ = kept_ref.shape
    core = core_ref[0]
    for y in range(blocks):
        for which, ref in ((core, kept_ref), (1 - core, given_ref)):
            at = pl.ds(pl.multiple_of((2 * y + which) * rows, rows), rows)
            ref[y] = (total[at, :] + own_ref[at, :]).astype(ref.dtype)


def product_cost(pair, feature_count):
    return pl.CostEstimate(
        flops=2 * pair.size * feature_count,
        bytes_accessed=2 * pair.shape[1] * feature_count + 8 * pair.shape[0] * feature_count,
        transcendentals=0,
    )


def own_input_terms(gate, up, pair):
    return pl.pallas_call(
        own_input_kernel,
        out_shape=jax.ShapeDtypeStruct((gate.shape[0], pair.shape[0]), F32),
        compiler_params=PARAMS,
        cost_estimate=product_cost(pair, gate.shape[0]),
    )(gate, up, pair)


def other_input_terms(core, gate, up, pair, own, out):
    feature_count, token_count = own.shape
    shape = (out // 2, feature_count // out, token_count)
    return pl.pallas_call(
        other_input_kernel,
        out_shape=(jax.ShapeDtypeStruct(shape, F32), jax.ShapeDtypeStruct(shape, BF16)),
        in_specs=[IN_SMEM] + [IN_VMEM] * 4,
        out_specs=(IN_VMEM, IN_VMEM),
        scratch_shapes=[pltpu.VMEM((feature_count, token_count), F32)],
        compiler_params=PARAMS,
        cost_estimate=product_cost(pair, feature_count),
    )(core, gate, up, pair, own)


def split_kernel(index_ref, kept_ref, received_ref, mine_ref, *sent_refs):
    for k, ref in enumerate((mine_ref, *sent_refs)):
        at = index_ref[0] ^ k
        ref[...] = (kept_ref[at] + received_ref[at].astype(F32)).astype(ref.dtype)


def split_shares(index, kept, received):
    shape = kept.shape[1:]
    others = kept.shape[0] - 1
    return pl.pallas_call(
        split_kernel,
        out_shape=[jax.ShapeDtypeStruct(shape, F32)] + [jax.ShapeDtypeStruct(shape, BF16)] * others,
        in_specs=[IN_SMEM, IN_VMEM, IN_VMEM],
        out_specs=[IN_VMEM] * (others + 1),
        compiler_params=PARAMS,
        cost_estimate=pl.CostEstimate(
            flops=2 * kept.size, bytes_accessed=10 * kept.size, transcendentals=0
        ),
    )(index, kept, received)


def weight_kernel(which, factor, tokens_ref, block_ref, out_ref):
    rows = out_ref.shape[0]
    total = lax.dot_general(
        tokens_ref[which * rows : (which + 1) * rows, :],
        block_ref[...],
        ROWS_BY_COLS,
        preferred_element_type=F32,
    )
    out_ref[...] = (total * factor).astype(BF16)


def weight_terms(tokens, which, block, factor):
    feature_count = tokens.shape[0] // 2
    token_count, width = block.shape
    return pl.pallas_call(
        functools.partial(weight_kernel, which, factor),
        out_shape=jax.ShapeDtypeStruct((feature_count, width), BF16),
        compiler_params=PARAMS,
        cost_estimate=pl.CostEstimate(
            flops=2 * token_count * feature_count * width,
            bytes_accessed=2 * token_count * (feature_count + width),
            transcendentals=0,
        ),
    )(tokens, block)


def finish_kernel(skips, side_ref, swapped_ref, gate_ref, up_ref):
    width = swapped_ref.shape[2] // 2
    half = gate_ref.shape[1] // 2
    blocks = len(skips)
    for u, out_ref in enumerate((gate_ref, up_ref)):
        for s in range(2):
            first = (side_ref[0] if s == 0 else 1 - side_ref[0]) * half
            for b, skip in enumerate(skips):
                at = pl.multiple_of(first + b * width, LANES)
                out_ref[:, pl.ds(at, width - skip)] = swapped_ref[u * blocks + b][
                    :, s * width + skip : (s + 1) * width
                ]


def finished(side, swapped, half, skips):
    shape = jax.ShapeDtypeStruct((swapped.shape[1], 2 * half), BF16)
    return pl.pallas_call(
        functools.partial(finish_kernel, skips),
        out_shape=(shape, shape),
        in_specs=[IN_SMEM, IN_VMEM],
        out_specs=(IN_VMEM, IN_VMEM),
        compiler_params=PARAMS,
        cost_estimate=pl.CostEstimate(
            flops=0, bytes_accessed=4 * swapped.size, transcendentals=0
        ),
    )(side, swapped)


def shards(tokens, grad_hidden, w_gate, w_up):
    token_count, feature_count = tokens.shape
    hidden = w_gate.shape[1]
    inp, out, dep = (lax.axis_size(name) for name in ("inp", "out", "dep"))
    factor = 1.0 / math.sqrt(token_count * dep)
    half = hidden // 2
    group = inp // 2
    rows = token_count // group
    pairs = [(i, i ^ 1) for i in range(inp)]
    alike = [[p + 2 * i for i in range(group)] for p in range(2)]
    place = lax.axis_index("inp")
    parity = place % 2
    own_side = parity.reshape(1)
    other_side = 1 - own_side

    theirs = lax.ppermute(tokens, "inp", pairs)
    given = partial_values(other_side, tokens, w_gate, w_up)
    kept = partial_values(own_side, tokens, w_gate, w_up)
    theirs, kept = lax.optimization_barrier((theirs, kept))
    two = jnp.concatenate([tokens, theirs], axis=1)
    all_tokens = lax.all_gather(two, "dep", axis=0, tiled=True)
    kept = kept.astype(F32) + lax.ppermute(given, "inp", pairs).astype(F32)
    kept, w_gate, w_up = lax.optimization_barrier((kept.astype(BF16), w_gate, w_up))
    terms = lax.all_to_all(
        kept.reshape(group, rows, hidden), "inp", 0, 0, axis_index_groups=alike
    )
    cotangent = lax.dynamic_slice(
        grad_hidden, ((place // 2) * rows, parity * half), (rows, half)
    )
    own_weights, other_weights = (
        [lax.dynamic_slice(w, (0, side * half), (feature_count, half)) for w in (w_gate, w_up)]
        for side in (parity, 1 - parity)
    )
    terms, own_weights, other_weights = lax.optimization_barrier(
        (terms, own_weights, other_weights)
    )
    own = lax.all_gather(
        grad_pair(terms, cotangent), "inp", axis=0, tiled=True, axis_index_groups=alike
    )
    other = lax.ppermute(own, "inp", pairs)

    width = 2 * LANES
    blocks = dep // 2
    starts = [min(b * width, half - width) for b in range(blocks)]
    skips = [b * width - s for b, s in enumerate(starts)]
    own_block = lax.all_to_all(dep_pieces(own, starts, width), "dep", 0, 0)
    own_block = own_block.reshape(dep * token_count, width)
    own_share = own_input_terms(*own_weights, own)
    own_block, across, own_share, other = lax.optimization_barrier(
        (own_block, all_tokens.T, own_share, other)
    )
    other_grad = lax.ppermute(weight_terms(across, 1, own_block, factor), "inp", pairs)
    own_grad = weight_terms(across, 0, own_block, factor)

    at_out = lax.axis_index("out")
    core = (at_out % 2).reshape(1)
    chip = (at_out // 2).reshape(1)
    kept, given = other_input_terms(core, *other_weights, other, own_share, out)
    received = lax.ppermute(given, "out", [(i, i ^ 1) for i in range(out)])
    own_grad, received = lax.optimization_barrier((own_grad, received))
    mine, *sent = split_shares(chip, kept, received)
    for k, block in enumerate(sent, 1):
        mine = mine + lax.ppermute(block, "out", [(i, i ^ 2 * k) for i in range(out)]).astype(F32)
    grad_input = mine.astype(BF16).T

    grad = jnp.concatenate([own_grad, other_grad], axis=1)
    swapped = lax.all_to_all(grad.reshape(dep, feature_count // dep, 2 * width), "dep", 0, 0)
    gate_grad, up_grad = finished(own_side, swapped, half, skips)
    return grad_input, gate_grad, up_grad


def solution(mesh):
    return jax.shard_map(
        shards,
        mesh=mesh,
        in_specs=(P("dep", "inp"), P("dep", "out"), P("inp", "out"), P("inp", "out")),
        out_specs=(P("dep", ("inp", "out")), P(("inp", "dep"), "out"), P(("inp", "dep"), "out")),
        check_vma=False,
    )
```

```python
import functools
import math

import jax
import jax.numpy as jnp
from jax import lax
from jax.experimental import pallas as pl
from jax.experimental.pallas import tpu as pltpu
from jax.sharding import PartitionSpec as P

BF16 = jnp.bfloat16
F32 = jnp.float32
LANES = 128
ROWS_BY_COLS = (((1,), (0,)), ((), ()))
COLS_BY_COLS = (((1,), (1,)), ((), ()))


def values_kernel(
    side_ref, tokens_hbm, gate_hbm, up_hbm, out_hbm, tokens_ref, gate_ref, up_ref, out_ref, sems
):
    half = gate_ref.shape[1]
    columns = pl.ds(pl.multiple_of(side_ref[0] * half, LANES), half)
    fetches = [
        pltpu.make_async_copy(tokens_hbm, tokens_ref, sems.at[0]),
        pltpu.make_async_copy(gate_hbm.at[:, columns], gate_ref, sems.at[1]),
        pltpu.make_async_copy(up_hbm.at[:, columns], up_ref, sems.at[2]),
    ]
    for fetch in fetches:
        fetch.start()
    fetches[0].wait()
    stores = []
    for u, w_ref in enumerate((gate_ref, up_ref)):
        fetches[1 + u].wait()
        part = lax.dot_general(
            tokens_ref[...], w_ref[...], ROWS_BY_COLS, preferred_element_type=F32
        )
        out_ref[u] = part.astype(out_ref.dtype)
        store = pltpu.make_async_copy(
            out_ref.at[u], out_hbm.at[:, pl.ds(u * half, half)], sems.at[3 + u]
        )
        store.start()
        stores.append(store)
    for store in stores:
        store.wait()


IN_HBM = pl.BlockSpec(memory_space=pltpu.HBM)
IN_SMEM = pl.BlockSpec(memory_space=pltpu.SMEM)
IN_VMEM = pl.BlockSpec(memory_space=pltpu.VMEM)
PARAMS = pltpu.CompilerParams(vmem_limit_bytes=16 * 2**20)
WHOLE = pltpu.CompilerParams(vmem_limit_bytes=60 * 2**20)


def partial_values(side, tokens, w_gate, w_up):
    token_count, feature_count = tokens.shape
    half = w_gate.shape[1] // 2
    return pl.pallas_call(
        values_kernel,
        out_shape=jax.ShapeDtypeStruct((token_count, 2 * half), BF16),
        in_specs=[IN_SMEM, IN_HBM, IN_HBM, IN_HBM],
        out_specs=IN_HBM,
        scratch_shapes=[
            pltpu.VMEM((token_count, feature_count), BF16),
            pltpu.VMEM((feature_count, half), BF16),
            pltpu.VMEM((feature_count, half), BF16),
            pltpu.VMEM((2, token_count, half), BF16),
            pltpu.SemaphoreType.DMA((5,)),
        ],
        compiler_params=WHOLE,
        cost_estimate=pl.CostEstimate(
            flops=4 * token_count * feature_count * half,
            bytes_accessed=4 * feature_count * half + 4 * token_count * half,
            transcendentals=0,
        ),
    )(side, tokens, w_gate, w_up)


def grads_kernel(terms_ref, cotangent_ref, pair_ref):
    half = cotangent_ref.shape[1]
    values = terms_ref[0].astype(F32)
    for k in range(1, terms_ref.shape[0]):
        values = values + terms_ref[k].astype(F32)
    gate_value = values[:, :half]
    up_value = values[:, half:]
    cotangent = cotangent_ref[...].astype(F32)
    sigmoid_gate = jax.nn.sigmoid(gate_value)
    grad_gate = cotangent * up_value * sigmoid_gate * (1.0 + gate_value * (1.0 - sigmoid_gate))
    grad_upper = cotangent * gate_value * sigmoid_gate
    pair_ref[:, :half] = grad_gate.astype(BF16)
    pair_ref[:, half:] = grad_upper.astype(BF16)


def grad_pair(terms, cotangent):
    rows, half = cotangent.shape
    return pl.pallas_call(
        grads_kernel,
        out_shape=jax.ShapeDtypeStruct((rows, 2 * half), BF16),
        compiler_params=PARAMS,
        cost_estimate=pl.CostEstimate(
            flops=40 * rows * half,
            bytes_accessed=2 * terms.size + 8 * rows * half,
            transcendentals=rows * half,
        ),
    )(terms, cotangent)


def pieces_kernel(starts, pair_ref, pieces_ref):
    half = pair_ref.shape[1] // 2
    width = pieces_ref.shape[2]
    for u in range(2):
        for b, start in enumerate(starts):
            first = u * half + start
            pieces_ref[u * len(starts) + b] = pair_ref[:, first : first + width]


def dep_pieces(pair, starts, width):
    shape = (2 * len(starts), pair.shape[0], width)
    return pl.pallas_call(
        functools.partial(pieces_kernel, starts),
        out_shape=jax.ShapeDtypeStruct(shape, BF16),
        compiler_params=pltpu.CompilerParams(vmem_limit_bytes=40 * 2**20),
        cost_estimate=pl.CostEstimate(
            flops=0, bytes_accessed=4 * math.prod(shape), transcendentals=0
        ),
    )(pair)


def own_input_kernel(gate_ref, up_ref, pair_ref, out_ref):
    half = gate_ref.shape[1]
    out_ref[...] = sum(
        lax.dot_general(
            w_ref[...],
            pair_ref[:, u * half : (u + 1) * half],
            COLS_BY_COLS,
            preferred_element_type=F32,
        )
        for u, w_ref in enumerate((gate_ref, up_ref))
    )


def other_input_kernel(gate_ref, up_ref, pair_ref, own_ref, out_ref):
    half = gate_ref.shape[1]
    total = own_ref[...]
    for u, w_ref in enumerate((gate_ref, up_ref)):
        total = total + lax.dot_general(
            w_ref[...],
            pair_ref[:, u * half : (u + 1) * half],
            COLS_BY_COLS,
            preferred_element_type=F32,
        )
    out_ref[...] = total.astype(BF16)


def product_cost(pair, feature_count):
    return pl.CostEstimate(
        flops=2 * pair.size * feature_count,
        bytes_accessed=2 * pair.shape[1] * feature_count + 8 * pair.shape[0] * feature_count,
        transcendentals=0,
    )


def own_input_terms(gate, up, pair):
    return pl.pallas_call(
        own_input_kernel,
        out_shape=jax.ShapeDtypeStruct((gate.shape[0], pair.shape[0]), F32),
        compiler_params=PARAMS,
        cost_estimate=product_cost(pair, gate.shape[0]),
    )(gate, up, pair)


def other_input_terms(gate, up, pair, own):
    return pl.pallas_call(
        other_input_kernel,
        out_shape=jax.ShapeDtypeStruct(own.shape, BF16),
        compiler_params=PARAMS,
        cost_estimate=product_cost(pair, own.shape[0]),
    )(gate, up, pair, own)


def weight_kernel(which, factor, tokens_ref, block_ref, out_ref):
    rows = out_ref.shape[0]
    total = lax.dot_general(
        tokens_ref[which * rows : (which + 1) * rows, :],
        block_ref[...],
        ROWS_BY_COLS,
        preferred_element_type=F32,
    )
    out_ref[...] = (total * factor).astype(BF16)


def weight_terms(tokens, which, block, factor):
    feature_count = tokens.shape[0] // 2
    token_count, width = block.shape
    return pl.pallas_call(
        functools.partial(weight_kernel, which, factor),
        out_shape=jax.ShapeDtypeStruct((feature_count, width), BF16),
        compiler_params=PARAMS,
        cost_estimate=pl.CostEstimate(
            flops=2 * token_count * feature_count * width,
            bytes_accessed=2 * token_count * (feature_count + width),
            transcendentals=0,
        ),
    )(tokens, block)


def finish_kernel(skips, side_ref, swapped_ref, gate_ref, up_ref):
    width = swapped_ref.shape[2] // 2
    half = gate_ref.shape[1] // 2
    blocks = len(skips)
    for u, out_ref in enumerate((gate_ref, up_ref)):
        for s in range(2):
            first = (side_ref[0] if s == 0 else 1 - side_ref[0]) * half
            for b, skip in enumerate(skips):
                at = pl.multiple_of(first + b * width, LANES)
                out_ref[:, pl.ds(at, width - skip)] = swapped_ref[u * blocks + b][
                    :, s * width + skip : (s + 1) * width
                ]


def finished(side, swapped, half, skips):
    shape = jax.ShapeDtypeStruct((swapped.shape[1], 2 * half), BF16)
    return pl.pallas_call(
        functools.partial(finish_kernel, skips),
        out_shape=(shape, shape),
        in_specs=[IN_SMEM, IN_VMEM],
        out_specs=(IN_VMEM, IN_VMEM),
        compiler_params=PARAMS,
        cost_estimate=pl.CostEstimate(
            flops=0, bytes_accessed=4 * swapped.size, transcendentals=0
        ),
    )(side, swapped)


def shards(tokens, grad_hidden, w_gate, w_up):
    token_count, feature_count = tokens.shape
    hidden = w_gate.shape[1]
    inp, out, dep = (lax.axis_size(name) for name in ("inp", "out", "dep"))
    factor = 1.0 / math.sqrt(token_count * dep)
    half = hidden // 2
    group = inp // 2
    rows = token_count // group
    pairs = [(i, i ^ 1) for i in range(inp)]
    alike = [[p + 2 * i for i in range(group)] for p in range(2)]
    place = lax.axis_index("inp")
    parity = place % 2
    own_side = parity.reshape(1)
    other_side = 1 - own_side

    given = partial_values(other_side, tokens, w_gate, w_up)
    own_side, given = lax.optimization_barrier((own_side, given))
    kept = partial_values(own_side, tokens, w_gate, w_up)
    mine, kept = lax.optimization_barrier((tokens, kept))
    theirs = lax.ppermute(mine, "inp", pairs)
    kept = kept.astype(F32) + lax.ppermute(given, "inp", pairs).astype(F32)
    kept, w_gate, w_up, theirs = lax.optimization_barrier((kept.astype(BF16), w_gate, w_up, theirs))
    two = jnp.concatenate([tokens, theirs], axis=1)
    all_tokens = lax.all_gather(two, "dep", axis=0, tiled=True)
    terms = lax.all_to_all(
        kept.reshape(group, rows, hidden), "inp", 0, 0, axis_index_groups=alike
    )
    cotangent = lax.dynamic_slice(
        grad_hidden, ((place // 2) * rows, parity * half), (rows, half)
    )
    own_weights, other_weights = (
        [lax.dynamic_slice(w, (0, side * half), (feature_count, half)) for w in (w_gate, w_up)]
        for side in (parity, 1 - parity)
    )
    terms, own_weights, other_weights = lax.optimization_barrier(
        (terms, own_weights, other_weights)
    )
    own = lax.all_gather(
        grad_pair(terms, cotangent), "inp", axis=0, tiled=True, axis_index_groups=alike
    )
    other = lax.ppermute(own, "inp", pairs)

    width = 2 * LANES
    blocks = dep // 2
    starts = [min(b * width, half - width) for b in range(blocks)]
    skips = [b * width - s for b, s in enumerate(starts)]
    own_block = lax.all_to_all(dep_pieces(own, starts, width), "dep", 0, 0)
    own_block = own_block.reshape(dep * token_count, width)
    own_share = own_input_terms(*own_weights, own)
    shares = other_input_terms(*other_weights, other, own_share)
    own_block, across, shares = lax.optimization_barrier((own_block, all_tokens.T, shares))
    other_grad = lax.ppermute(weight_terms(across, 1, own_block, factor), "inp", pairs)
    own_grad = weight_terms(across, 0, own_block, factor)
    shares = lax.all_to_all(
        shares.reshape(out, feature_count // out, token_count), "out", 0, 0
    )
    grad_input = jnp.sum(shares.astype(F32), axis=0).astype(BF16).T

    grad = jnp.concatenate([own_grad, other_grad], axis=1)
    swapped = lax.all_to_all(grad.reshape(dep, feature_count // dep, 2 * width), "dep", 0, 0)
    gate_grad, up_grad = finished(own_side, swapped, half, skips)
    return grad_input, gate_grad, up_grad


def solution(mesh):
    return jax.shard_map(
        shards,
        mesh=mesh,
        in_specs=(P("dep", "inp"), P("dep", "out"), P("inp", "out"), P("inp", "out")),
        out_specs=(P("dep", ("inp", "out")), P(("inp", "dep"), "out"), P(("inp", "dep"), "out")),
        check_vma=False,
    )
```

```python
import functools
import math

import jax
import jax.numpy as jnp
from jax import lax
from jax.experimental import pallas as pl
from jax.experimental.pallas import tpu as pltpu
from jax.sharding import PartitionSpec as P

BF16 = jnp.bfloat16
F32 = jnp.float32
LANES = 128
ROWS_BY_COLS = (((1,), (0,)), ((), ()))
COLS_BY_COLS = (((1,), (1,)), ((), ()))


def values_kernel(
    side_ref, tokens_hbm, gate_hbm, up_hbm, out_hbm, tokens_ref, gate_ref, up_ref, out_ref, sems
):
    half = gate_ref.shape[1]
    columns = pl.ds(pl.multiple_of(side_ref[0] * half, LANES), half)
    fetches = [
        pltpu.make_async_copy(tokens_hbm, tokens_ref, sems.at[0]),
        pltpu.make_async_copy(gate_hbm.at[:, columns], gate_ref, sems.at[1]),
        pltpu.make_async_copy(up_hbm.at[:, columns], up_ref, sems.at[2]),
    ]
    for fetch in fetches:
        fetch.start()
    fetches[0].wait()
    stores = []
    for u, w_ref in enumerate((gate_ref, up_ref)):
        fetches[1 + u].wait()
        part = lax.dot_general(
            tokens_ref[...], w_ref[...], ROWS_BY_COLS, preferred_element_type=F32
        )
        out_ref[u] = part.astype(out_ref.dtype)
        store = pltpu.make_async_copy(
            out_ref.at[u], out_hbm.at[:, pl.ds(u * half, half)], sems.at[3 + u]
        )
        store.start()
        stores.append(store)
    for store in stores:
        store.wait()


IN_HBM = pl.BlockSpec(memory_space=pltpu.HBM)
IN_SMEM = pl.BlockSpec(memory_space=pltpu.SMEM)
IN_VMEM = pl.BlockSpec(memory_space=pltpu.VMEM)
PARAMS = pltpu.CompilerParams(vmem_limit_bytes=16 * 2**20)
WHOLE = pltpu.CompilerParams(vmem_limit_bytes=60 * 2**20)


def partial_values(side, tokens, w_gate, w_up):
    token_count, feature_count = tokens.shape
    half = w_gate.shape[1] // 2
    return pl.pallas_call(
        values_kernel,
        out_shape=jax.ShapeDtypeStruct((token_count, 2 * half), BF16),
        in_specs=[IN_SMEM, IN_HBM, IN_HBM, IN_HBM],
        out_specs=IN_HBM,
        scratch_shapes=[
            pltpu.VMEM((token_count, feature_count), BF16),
            pltpu.VMEM((feature_count, half), BF16),
            pltpu.VMEM((feature_count, half), BF16),
            pltpu.VMEM((2, token_count, half), BF16),
            pltpu.SemaphoreType.DMA((5,)),
        ],
        compiler_params=WHOLE,
        cost_estimate=pl.CostEstimate(
            flops=4 * token_count * feature_count * half,
            bytes_accessed=4 * feature_count * half + 4 * token_count * half,
            transcendentals=0,
        ),
    )(side, tokens, w_gate, w_up)


def grads_kernel(terms_ref, cotangent_ref, pair_ref):
    half = cotangent_ref.shape[1]
    values = terms_ref[0].astype(F32)
    for k in range(1, terms_ref.shape[0]):
        values = values + terms_ref[k].astype(F32)
    gate_value = values[:, :half]
    up_value = values[:, half:]
    cotangent = cotangent_ref[...].astype(F32)
    sigmoid_gate = jax.nn.sigmoid(gate_value)
    grad_gate = cotangent * up_value * sigmoid_gate * (1.0 + gate_value * (1.0 - sigmoid_gate))
    grad_upper = cotangent * gate_value * sigmoid_gate
    pair_ref[:, :half] = grad_gate.astype(BF16)
    pair_ref[:, half:] = grad_upper.astype(BF16)


def grad_pair(terms, cotangent):
    rows, half = cotangent.shape
    return pl.pallas_call(
        grads_kernel,
        out_shape=jax.ShapeDtypeStruct((rows, 2 * half), BF16),
        compiler_params=PARAMS,
        cost_estimate=pl.CostEstimate(
            flops=40 * rows * half,
            bytes_accessed=2 * terms.size + 8 * rows * half,
            transcendentals=rows * half,
        ),
    )(terms, cotangent)


def pieces_kernel(starts, pair_ref, pieces_ref):
    half = pair_ref.shape[1] // 2
    width = pieces_ref.shape[2]
    for u in range(2):
        for b, start in enumerate(starts):
            first = u * half + start
            pieces_ref[u * len(starts) + b] = pair_ref[:, first : first + width]


def dep_pieces(pair, starts, width):
    shape = (2 * len(starts), pair.shape[0], width)
    return pl.pallas_call(
        functools.partial(pieces_kernel, starts),
        out_shape=jax.ShapeDtypeStruct(shape, BF16),
        compiler_params=pltpu.CompilerParams(vmem_limit_bytes=40 * 2**20),
        cost_estimate=pl.CostEstimate(
            flops=0, bytes_accessed=4 * math.prod(shape), transcendentals=0
        ),
    )(pair)


def own_input_kernel(gate_ref, up_ref, pair_ref, out_ref):
    half = gate_ref.shape[1]
    out_ref[...] = sum(
        lax.dot_general(
            w_ref[...],
            pair_ref[:, u * half : (u + 1) * half],
            COLS_BY_COLS,
            preferred_element_type=F32,
        )
        for u, w_ref in enumerate((gate_ref, up_ref))
    )


def other_input_kernel(gate_ref, up_ref, pair_ref, own_ref, out_ref):
    half = gate_ref.shape[1]
    total = own_ref[...]
    for u, w_ref in enumerate((gate_ref, up_ref)):
        total = total + lax.dot_general(
            w_ref[...],
            pair_ref[:, u * half : (u + 1) * half],
            COLS_BY_COLS,
            preferred_element_type=F32,
        )
    out_ref[...] = total.astype(BF16)


def product_cost(pair, feature_count):
    return pl.CostEstimate(
        flops=2 * pair.size * feature_count,
        bytes_accessed=2 * pair.shape[1] * feature_count + 8 * pair.shape[0] * feature_count,
        transcendentals=0,
    )


def own_input_terms(gate, up, pair):
    return pl.pallas_call(
        own_input_kernel,
        out_shape=jax.ShapeDtypeStruct((gate.shape[0], pair.shape[0]), F32),
        compiler_params=PARAMS,
        cost_estimate=product_cost(pair, gate.shape[0]),
    )(gate, up, pair)


def other_input_terms(gate, up, pair, own):
    return pl.pallas_call(
        other_input_kernel,
        out_shape=jax.ShapeDtypeStruct(own.shape, BF16),
        compiler_params=PARAMS,
        cost_estimate=product_cost(pair, own.shape[0]),
    )(gate, up, pair, own)


def across_kernel(mine_ref, theirs_ref, out_ref):
    rows = mine_ref.shape[1]
    out_ref[:rows, :] = mine_ref[...].astype(F32).T.astype(BF16)
    out_ref[rows:, :] = theirs_ref[...].astype(F32).T.astype(BF16)


def features_by_tokens(mine, theirs):
    token_count, feature_count = mine.shape
    return pl.pallas_call(
        across_kernel,
        out_shape=jax.ShapeDtypeStruct((2 * feature_count, token_count), BF16),
        compiler_params=PARAMS,
        cost_estimate=pl.CostEstimate(flops=0, bytes_accessed=8 * mine.size, transcendentals=0),
    )(mine, theirs)


def weight_kernel(factor, tokens_ref, block_ref, out_ref, total_ref):
    step = pl.program_id(0)
    term = lax.dot_general(
        tokens_ref[0], block_ref[0], ROWS_BY_COLS, preferred_element_type=F32
    )
    for more in range(1, tokens_ref.shape[0]):
        term = term + lax.dot_general(
            tokens_ref[more], block_ref[more], ROWS_BY_COLS, preferred_element_type=F32
        )

    @pl.when(step == 0)
    def _():
        total_ref[...] = term

    @pl.when(step > 0)
    def _():
        total_ref[...] += term

    @pl.when(step == pl.num_programs(0) - 1)
    def _():
        out_ref[...] = (total_ref[...] * factor).astype(BF16)


def weight_terms(tokens, which, block, factor):
    dep, token_count, width = block.shape
    feature_count = tokens.shape[1] // 2
    return pl.pallas_call(
        functools.partial(weight_kernel, factor),
        out_shape=jax.ShapeDtypeStruct((feature_count, width), BF16),
        grid=(dep // 2,),
        in_specs=[
            pl.BlockSpec((2, feature_count, token_count), lambda d: (d, which, 0)),
            pl.BlockSpec((2, token_count, width), lambda d: (d, 0, 0)),
        ],
        out_specs=pl.BlockSpec((feature_count, width), lambda d: (0, 0)),
        scratch_shapes=[pltpu.VMEM((feature_count, width), F32)],
        compiler_params=WHOLE,
        cost_estimate=pl.CostEstimate(
            flops=2 * dep * token_count * feature_count * width,
            bytes_accessed=2 * dep * token_count * (feature_count + width),
            transcendentals=0,
        ),
    )(tokens, block)


def finish_kernel(skips, side_ref, swapped_ref, gate_ref, up_ref):
    width = swapped_ref.shape[2] // 2
    half = gate_ref.shape[1] // 2
    blocks = len(skips)
    for u, out_ref in enumerate((gate_ref, up_ref)):
        for s in range(2):
            first = (side_ref[0] if s == 0 else 1 - side_ref[0]) * half
            for b, skip in enumerate(skips):
                at = pl.multiple_of(first + b * width, LANES)
                out_ref[:, pl.ds(at, width - skip)] = swapped_ref[u * blocks + b][
                    :, s * width + skip : (s + 1) * width
                ]


def finished(side, swapped, half, skips):
    shape = jax.ShapeDtypeStruct((swapped.shape[1], 2 * half), BF16)
    return pl.pallas_call(
        functools.partial(finish_kernel, skips),
        out_shape=(shape, shape),
        in_specs=[IN_SMEM, IN_VMEM],
        out_specs=(IN_VMEM, IN_VMEM),
        compiler_params=PARAMS,
        cost_estimate=pl.CostEstimate(
            flops=0, bytes_accessed=4 * swapped.size, transcendentals=0
        ),
    )(side, swapped)


def shards(tokens, grad_hidden, w_gate, w_up):
    token_count, feature_count = tokens.shape
    hidden = w_gate.shape[1]
    inp, out, dep = (lax.axis_size(name) for name in ("inp", "out", "dep"))
    factor = 1.0 / math.sqrt(token_count * dep)
    half = hidden // 2
    group = inp // 2
    rows = token_count // group
    pairs = [(i, i ^ 1) for i in range(inp)]
    alike = [[p + 2 * i for i in range(group)] for p in range(2)]
    place = lax.axis_index("inp")
    parity = place % 2
    own_side = parity.reshape(1)
    other_side = 1 - own_side

    given = partial_values(other_side, tokens, w_gate, w_up)
    own_side, given = lax.optimization_barrier((own_side, given))
    kept = partial_values(own_side, tokens, w_gate, w_up)
    mine, kept = lax.optimization_barrier((tokens, kept))
    theirs = lax.ppermute(mine, "inp", pairs)
    kept = kept.astype(F32) + lax.ppermute(given, "inp", pairs).astype(F32)
    kept, w_gate, w_up, theirs = lax.optimization_barrier((kept.astype(BF16), w_gate, w_up, theirs))
    across = lax.all_gather(features_by_tokens(tokens, theirs), "dep", axis=0)
    terms = lax.all_to_all(
        kept.reshape(group, rows, hidden), "inp", 0, 0, axis_index_groups=alike
    )
    cotangent = lax.dynamic_slice(
        grad_hidden, ((place // 2) * rows, parity * half), (rows, half)
    )
    own_weights, other_weights = (
        [lax.dynamic_slice(w, (0, side * half), (feature_count, half)) for w in (w_gate, w_up)]
        for side in (parity, 1 - parity)
    )
    terms, own_weights, other_weights = lax.optimization_barrier(
        (terms, own_weights, other_weights)
    )
    own = lax.all_gather(
        grad_pair(terms, cotangent), "inp", axis=0, tiled=True, axis_index_groups=alike
    )
    other = lax.ppermute(own, "inp", pairs)

    width = 2 * LANES
    blocks = dep // 2
    starts = [min(b * width, half - width) for b in range(blocks)]
    skips = [b * width - s for b, s in enumerate(starts)]
    own_block = lax.all_to_all(dep_pieces(own, starts, width), "dep", 0, 0)
    own_share = own_input_terms(*own_weights, own)
    shares = other_input_terms(*other_weights, other, own_share)
    own_block, shares = lax.optimization_barrier((own_block, shares))
    other_grad = lax.ppermute(weight_terms(across, 1, own_block, factor), "inp", pairs)
    own_grad = weight_terms(across, 0, own_block, factor)
    shares = lax.all_to_all(
        shares.reshape(out, feature_count // out, token_count), "out", 0, 0
    )
    grad_input = jnp.sum(shares.astype(F32), axis=0).astype(BF16).T

    grad = jnp.concatenate([own_grad, other_grad], axis=1)
    swapped = lax.all_to_all(grad.reshape(dep, feature_count // dep, 2 * width), "dep", 0, 0)
    gate_grad, up_grad = finished(own_side, swapped, half, skips)
    return grad_input, gate_grad, up_grad


def solution(mesh):
    return jax.shard_map(
        shards,
        mesh=mesh,
        in_specs=(P("dep", "inp"), P("dep", "out"), P("inp", "out"), P("inp", "out")),
        out_specs=(P("dep", ("inp", "out")), P(("inp", "dep"), "out"), P(("inp", "dep"), "out")),
        check_vma=False,
    )
```

```python
import functools
import math

import jax
import jax.numpy as jnp
from jax import lax
from jax.experimental import pallas as pl
from jax.experimental.pallas import tpu as pltpu
from jax.sharding import PartitionSpec as P

BF16 = jnp.bfloat16
F32 = jnp.float32
LANES = 128
ROWS_BY_COLS = (((1,), (0,)), ((), ()))
COLS_BY_COLS = (((1,), (1,)), ((), ()))


def values_kernel(
    side_ref, tokens_hbm, gate_hbm, up_hbm, out_hbm, tokens_ref, gate_ref, up_ref, out_ref, sems
):
    half = gate_ref.shape[1]
    columns = pl.ds(pl.multiple_of(side_ref[0] * half, LANES), half)
    fetches = [
        pltpu.make_async_copy(tokens_hbm, tokens_ref, sems.at[0]),
        pltpu.make_async_copy(gate_hbm.at[:, columns], gate_ref, sems.at[1]),
        pltpu.make_async_copy(up_hbm.at[:, columns], up_ref, sems.at[2]),
    ]
    for fetch in fetches:
        fetch.start()
    fetches[0].wait()
    stores = []
    for u, w_ref in enumerate((gate_ref, up_ref)):
        fetches[1 + u].wait()
        part = lax.dot_general(
            tokens_ref[...], w_ref[...], ROWS_BY_COLS, preferred_element_type=F32
        )
        out_ref[u] = part.astype(out_ref.dtype)
        store = pltpu.make_async_copy(
            out_ref.at[u], out_hbm.at[:, pl.ds(u * half, half)], sems.at[3 + u]
        )
        store.start()
        stores.append(store)
    for store in stores:
        store.wait()


IN_HBM = pl.BlockSpec(memory_space=pltpu.HBM)
IN_SMEM = pl.BlockSpec(memory_space=pltpu.SMEM)
IN_VMEM = pl.BlockSpec(memory_space=pltpu.VMEM)
PARAMS = pltpu.CompilerParams(vmem_limit_bytes=16 * 2**20)
WHOLE = pltpu.CompilerParams(vmem_limit_bytes=60 * 2**20)


def partial_values(side, tokens, w_gate, w_up):
    token_count, feature_count = tokens.shape
    half = w_gate.shape[1] // 2
    return pl.pallas_call(
        values_kernel,
        out_shape=jax.ShapeDtypeStruct((token_count, 2 * half), BF16),
        in_specs=[IN_SMEM, IN_HBM, IN_HBM, IN_HBM],
        out_specs=IN_HBM,
        scratch_shapes=[
            pltpu.VMEM((token_count, feature_count), BF16),
            pltpu.VMEM((feature_count, half), BF16),
            pltpu.VMEM((feature_count, half), BF16),
            pltpu.VMEM((2, token_count, half), BF16),
            pltpu.SemaphoreType.DMA((5,)),
        ],
        compiler_params=WHOLE,
        cost_estimate=pl.CostEstimate(
            flops=4 * token_count * feature_count * half,
            bytes_accessed=4 * feature_count * half + 4 * token_count * half,
            transcendentals=0,
        ),
    )(side, tokens, w_gate, w_up)


def grads_kernel(terms_ref, cotangent_ref, pair_ref):
    half = cotangent_ref.shape[1]
    values = terms_ref[0].astype(F32)
    for k in range(1, terms_ref.shape[0]):
        values = values + terms_ref[k].astype(F32)
    gate_value = values[:, :half]
    up_value = values[:, half:]
    cotangent = cotangent_ref[...].astype(F32)
    sigmoid_gate = jax.nn.sigmoid(gate_value)
    grad_gate = cotangent * up_value * sigmoid_gate * (1.0 + gate_value * (1.0 - sigmoid_gate))
    grad_upper = cotangent * gate_value * sigmoid_gate
    pair_ref[:, :half] = grad_gate.astype(BF16)
    pair_ref[:, half:] = grad_upper.astype(BF16)


def grad_pair(terms, cotangent):
    rows, half = cotangent.shape
    return pl.pallas_call(
        grads_kernel,
        out_shape=jax.ShapeDtypeStruct((rows, 2 * half), BF16),
        compiler_params=PARAMS,
        cost_estimate=pl.CostEstimate(
            flops=40 * rows * half,
            bytes_accessed=2 * terms.size + 8 * rows * half,
            transcendentals=rows * half,
        ),
    )(terms, cotangent)


def pieces_kernel(starts, pair_ref, pieces_ref):
    half = pair_ref.shape[1] // 2
    width = pieces_ref.shape[2]
    for u in range(2):
        for b, start in enumerate(starts):
            first = u * half + start
            pieces_ref[u * len(starts) + b] = pair_ref[:, first : first + width]


def dep_pieces(pair, starts, width):
    shape = (2 * len(starts), pair.shape[0], width)
    return pl.pallas_call(
        functools.partial(pieces_kernel, starts),
        out_shape=jax.ShapeDtypeStruct(shape, BF16),
        compiler_params=pltpu.CompilerParams(vmem_limit_bytes=40 * 2**20),
        cost_estimate=pl.CostEstimate(
            flops=0, bytes_accessed=4 * math.prod(shape), transcendentals=0
        ),
    )(pair)


def own_input_kernel(gate_ref, up_ref, pair_ref, out_ref):
    half = gate_ref.shape[1]
    out_ref[...] = sum(
        lax.dot_general(
            w_ref[...],
            pair_ref[:, u * half : (u + 1) * half],
            COLS_BY_COLS,
            preferred_element_type=F32,
        )
        for u, w_ref in enumerate((gate_ref, up_ref))
    )


def other_input_kernel(gate_ref, up_ref, pair_ref, own_ref, out_ref):
    half = gate_ref.shape[1]
    total = own_ref[...]
    for u, w_ref in enumerate((gate_ref, up_ref)):
        total = total + lax.dot_general(
            w_ref[...],
            pair_ref[:, u * half : (u + 1) * half],
            COLS_BY_COLS,
            preferred_element_type=F32,
        )
    out_ref[...] = total.astype(BF16)


def product_cost(pair, feature_count):
    return pl.CostEstimate(
        flops=2 * pair.size * feature_count,
        bytes_accessed=2 * pair.shape[1] * feature_count + 8 * pair.shape[0] * feature_count,
        transcendentals=0,
    )


def own_input_terms(gate, up, pair):
    return pl.pallas_call(
        own_input_kernel,
        out_shape=jax.ShapeDtypeStruct((gate.shape[0], pair.shape[0]), F32),
        compiler_params=PARAMS,
        cost_estimate=product_cost(pair, gate.shape[0]),
    )(gate, up, pair)


def other_input_terms(gate, up, pair, own):
    return pl.pallas_call(
        other_input_kernel,
        out_shape=jax.ShapeDtypeStruct(own.shape, BF16),
        compiler_params=PARAMS,
        cost_estimate=product_cost(pair, own.shape[0]),
    )(gate, up, pair, own)


def across_kernel(tokens_ref, out_ref):
    out_ref[...] = tokens_ref[...].astype(F32).T.astype(BF16)


def features_by_tokens(tokens):
    return pl.pallas_call(
        across_kernel,
        out_shape=jax.ShapeDtypeStruct(tokens.shape[::-1], BF16),
        compiler_params=PARAMS,
        cost_estimate=pl.CostEstimate(flops=0, bytes_accessed=4 * tokens.size, transcendentals=0),
    )(tokens)


def weight_kernel(factor, tokens_ref, own_ref, other_ref, out_ref, total_ref):
    step = pl.program_id(0)
    terms = []
    for block_ref in (own_ref, other_ref):
        terms.append(
            sum(
                lax.dot_general(
                    tokens_ref[k], block_ref[k], ROWS_BY_COLS, preferred_element_type=F32
                )
                for k in range(tokens_ref.shape[0])
            )
        )

    @pl.when(step == 0)
    def _():
        for side, term in enumerate(terms):
            total_ref[side] = term

    @pl.when(step > 0)
    def _():
        for side, term in enumerate(terms):
            total_ref[side] += term

    @pl.when(step == pl.num_programs(0) - 1)
    def _():
        width = total_ref.shape[2]
        for side in range(2):
            out_ref[:, side * width : (side + 1) * width] = (total_ref[side] * factor).astype(BF16)


def weight_terms(tokens, own, other, factor):
    dep, feature_count, token_count = tokens.shape
    width = own.shape[2]
    steps = 4
    block = pl.BlockSpec((dep // steps, token_count, width), lambda d: (d, 0, 0))
    return pl.pallas_call(
        functools.partial(weight_kernel, factor),
        out_shape=jax.ShapeDtypeStruct((feature_count, 2 * width), BF16),
        grid=(steps,),
        in_specs=[
            pl.BlockSpec((dep // steps, feature_count, token_count), lambda d: (d, 0, 0)),
            block,
            block,
        ],
        out_specs=pl.BlockSpec((feature_count, 2 * width), lambda d: (0, 0)),
        scratch_shapes=[pltpu.VMEM((2, feature_count, width), F32)],
        compiler_params=WHOLE,
        cost_estimate=pl.CostEstimate(
            flops=4 * dep * token_count * feature_count * width,
            bytes_accessed=2 * dep * token_count * (feature_count + 2 * width),
            transcendentals=0,
        ),
    )(tokens, own, other)


def finish_kernel(skips, side_ref, swapped_ref, gate_ref, up_ref):
    width = swapped_ref.shape[2] // 2
    half = gate_ref.shape[1] // 2
    blocks = len(skips)
    for u, out_ref in enumerate((gate_ref, up_ref)):
        for s in range(2):
            first = (side_ref[0] if s == 0 else 1 - side_ref[0]) * half
            for b, skip in enumerate(skips):
                at = pl.multiple_of(first + b * width, LANES)
                out_ref[:, pl.ds(at, width - skip)] = swapped_ref[u * blocks + b][
                    :, s * width + skip : (s + 1) * width
                ]


def finished(side, swapped, half, skips):
    shape = jax.ShapeDtypeStruct((swapped.shape[1], 2 * half), BF16)
    return pl.pallas_call(
        functools.partial(finish_kernel, skips),
        out_shape=(shape, shape),
        in_specs=[IN_SMEM, IN_VMEM],
        out_specs=(IN_VMEM, IN_VMEM),
        compiler_params=PARAMS,
        cost_estimate=pl.CostEstimate(
            flops=0, bytes_accessed=4 * swapped.size, transcendentals=0
        ),
    )(side, swapped)


def shards(tokens, grad_hidden, w_gate, w_up):
    token_count, feature_count = tokens.shape
    hidden = w_gate.shape[1]
    inp, out, dep = (lax.axis_size(name) for name in ("inp", "out", "dep"))
    factor = 1.0 / math.sqrt(token_count * dep)
    half = hidden // 2
    group = inp // 2
    rows = token_count // group
    pairs = [(i, i ^ 1) for i in range(inp)]
    alike = [[p + 2 * i for i in range(group)] for p in range(2)]
    place = lax.axis_index("inp")
    parity = place % 2
    own_side = parity.reshape(1)
    other_side = 1 - own_side

    given = partial_values(other_side, tokens, w_gate, w_up)
    own_side, given = lax.optimization_barrier((own_side, given))
    kept = partial_values(own_side, tokens, w_gate, w_up)
    kept = kept.astype(F32) + lax.ppermute(given, "inp", pairs).astype(F32)
    kept, w_gate, w_up, tokens = lax.optimization_barrier(
        (kept.astype(BF16), w_gate, w_up, tokens)
    )
    across = lax.all_gather(features_by_tokens(tokens), "dep", axis=0)
    terms = lax.all_to_all(
        kept.reshape(group, rows, hidden), "inp", 0, 0, axis_index_groups=alike
    )
    cotangent = lax.dynamic_slice(
        grad_hidden, ((place // 2) * rows, parity * half), (rows, half)
    )
    own_weights, other_weights = (
        [lax.dynamic_slice(w, (0, side * half), (feature_count, half)) for w in (w_gate, w_up)]
        for side in (parity, 1 - parity)
    )
    terms, own_weights, other_weights = lax.optimization_barrier(
        (terms, own_weights, other_weights)
    )
    own = lax.all_gather(
        grad_pair(terms, cotangent), "inp", axis=0, tiled=True, axis_index_groups=alike
    )
    other = lax.ppermute(own, "inp", pairs)

    width = 2 * LANES
    blocks = dep // 2
    starts = [min(b * width, half - width) for b in range(blocks)]
    skips = [b * width - s for b, s in enumerate(starts)]
    own_block = lax.all_to_all(dep_pieces(own, starts, width), "dep", 0, 0)
    own_share = own_input_terms(*own_weights, own)
    own_block, own_share = lax.optimization_barrier((own_block, own_share))
    other_block = lax.ppermute(own_block, "inp", pairs)

    shares = other_input_terms(*other_weights, other, own_share)
    shares = lax.all_to_all(
        shares.reshape(out, feature_count // out, token_count), "out", 0, 0
    )
    grad_input = jnp.sum(shares.astype(F32), axis=0).astype(BF16).T

    grad = weight_terms(across, own_block, other_block, factor)
    swapped = lax.all_to_all(grad.reshape(dep, feature_count // dep, 2 * width), "dep", 0, 0)
    gate_grad, up_grad = finished(own_side, swapped, half, skips)
    return grad_input, gate_grad, up_grad


def solution(mesh):
    return jax.shard_map(
        shards,
        mesh=mesh,
        in_specs=(P("dep", "inp"), P("dep", "out"), P("inp", "out"), P("inp", "out")),
        out_specs=(P("dep", ("inp", "out")), P(("inp", "dep"), "out"), P(("inp", "dep"), "out")),
        check_vma=False,
    )
```

```python
import functools
import math

import jax
import jax.numpy as jnp
from jax import lax
from jax.experimental import pallas as pl
from jax.experimental.pallas import tpu as pltpu
from jax.sharding import PartitionSpec as P

BF16 = jnp.bfloat16
F32 = jnp.float32
LANES = 128
ROWS_BY_COLS = (((1,), (0,)), ((), ()))
COLS_BY_COLS = (((1,), (1,)), ((), ()))


def values_kernel(
    side_ref, tokens_hbm, gate_hbm, up_hbm, out_hbm, tokens_ref, gate_ref, up_ref, out_ref, sems
):
    half = gate_ref.shape[1]
    columns = pl.ds(pl.multiple_of(side_ref[0] * half, LANES), half)
    fetches = [
        pltpu.make_async_copy(tokens_hbm, tokens_ref, sems.at[0]),
        pltpu.make_async_copy(gate_hbm.at[:, columns], gate_ref, sems.at[1]),
        pltpu.make_async_copy(up_hbm.at[:, columns], up_ref, sems.at[2]),
    ]
    for fetch in fetches:
        fetch.start()
    fetches[0].wait()
    stores = []
    for u, w_ref in enumerate((gate_ref, up_ref)):
        fetches[1 + u].wait()
        part = lax.dot_general(
            tokens_ref[...], w_ref[...], ROWS_BY_COLS, preferred_element_type=F32
        )
        out_ref[u] = part.astype(out_ref.dtype)
        store = pltpu.make_async_copy(
            out_ref.at[u], out_hbm.at[:, pl.ds(u * half, half)], sems.at[3 + u]
        )
        store.start()
        stores.append(store)
    for store in stores:
        store.wait()


IN_HBM = pl.BlockSpec(memory_space=pltpu.HBM)
IN_SMEM = pl.BlockSpec(memory_space=pltpu.SMEM)
IN_VMEM = pl.BlockSpec(memory_space=pltpu.VMEM)
PARAMS = pltpu.CompilerParams(vmem_limit_bytes=16 * 2**20)
WHOLE = pltpu.CompilerParams(vmem_limit_bytes=60 * 2**20)


def partial_values(side, tokens, w_gate, w_up):
    token_count, feature_count = tokens.shape
    half = w_gate.shape[1] // 2
    return pl.pallas_call(
        values_kernel,
        out_shape=jax.ShapeDtypeStruct((token_count, 2 * half), BF16),
        in_specs=[IN_SMEM, IN_HBM, IN_HBM, IN_HBM],
        out_specs=IN_HBM,
        scratch_shapes=[
            pltpu.VMEM((token_count, feature_count), BF16),
            pltpu.VMEM((feature_count, half), BF16),
            pltpu.VMEM((feature_count, half), BF16),
            pltpu.VMEM((2, token_count, half), BF16),
            pltpu.SemaphoreType.DMA((5,)),
        ],
        compiler_params=WHOLE,
        cost_estimate=pl.CostEstimate(
            flops=4 * token_count * feature_count * half,
            bytes_accessed=4 * feature_count * half + 4 * token_count * half,
            transcendentals=0,
        ),
    )(side, tokens, w_gate, w_up)


def grads_kernel(terms_ref, cotangent_ref, pair_ref):
    half = cotangent_ref.shape[1]
    values = terms_ref[0].astype(F32)
    for k in range(1, terms_ref.shape[0]):
        values = values + terms_ref[k].astype(F32)
    gate_value = values[:, :half]
    up_value = values[:, half:]
    cotangent = cotangent_ref[...].astype(F32)
    sigmoid_gate = jax.nn.sigmoid(gate_value)
    grad_gate = cotangent * up_value * sigmoid_gate * (1.0 + gate_value * (1.0 - sigmoid_gate))
    grad_upper = cotangent * gate_value * sigmoid_gate
    pair_ref[:, :half] = grad_gate.astype(BF16)
    pair_ref[:, half:] = grad_upper.astype(BF16)


def grad_pair(terms, cotangent):
    rows, half = cotangent.shape
    return pl.pallas_call(
        grads_kernel,
        out_shape=jax.ShapeDtypeStruct((rows, 2 * half), BF16),
        compiler_params=PARAMS,
        cost_estimate=pl.CostEstimate(
            flops=40 * rows * half,
            bytes_accessed=2 * terms.size + 8 * rows * half,
            transcendentals=rows * half,
        ),
    )(terms, cotangent)


def pieces_kernel(starts, pair_ref, pieces_ref):
    half = pair_ref.shape[1] // 2
    width = pieces_ref.shape[2]
    for u in range(2):
        for b, start in enumerate(starts):
            first = u * half + start
            pieces_ref[u * len(starts) + b] = pair_ref[:, first : first + width]


def dep_pieces(pair, starts, width):
    shape = (2 * len(starts), pair.shape[0], width)
    return pl.pallas_call(
        functools.partial(pieces_kernel, starts),
        out_shape=jax.ShapeDtypeStruct(shape, BF16),
        compiler_params=pltpu.CompilerParams(vmem_limit_bytes=40 * 2**20),
        cost_estimate=pl.CostEstimate(
            flops=0, bytes_accessed=4 * math.prod(shape), transcendentals=0
        ),
    )(pair)


def own_input_kernel(gate_ref, up_ref, pair_ref, out_ref):
    half = gate_ref.shape[1]
    out_ref[...] = sum(
        lax.dot_general(
            w_ref[...],
            pair_ref[:, u * half : (u + 1) * half],
            COLS_BY_COLS,
            preferred_element_type=F32,
        )
        for u, w_ref in enumerate((gate_ref, up_ref))
    )


def other_input_kernel(core_ref, gate_ref, up_ref, pair_ref, own_ref, kept_ref, given_ref, total):
    own_input_kernel(gate_ref, up_ref, pair_ref, total)
    blocks, rows, _ = kept_ref.shape
    core = core_ref[0]
    for y in range(blocks):
        for which, ref in ((core, kept_ref), (1 - core, given_ref)):
            at = pl.ds(pl.multiple_of((2 * y + which) * rows, rows), rows)
            ref[y] = (total[at, :] + own_ref[at, :]).astype(ref.dtype)


def product_cost(pair, feature_count):
    return pl.CostEstimate(
        flops=2 * pair.size * feature_count,
        bytes_accessed=2 * pair.shape[1] * feature_count + 8 * pair.shape[0] * feature_count,
        transcendentals=0,
    )


def own_input_terms(gate, up, pair):
    return pl.pallas_call(
        own_input_kernel,
        out_shape=jax.ShapeDtypeStruct((gate.shape[0], pair.shape[0]), F32),
        compiler_params=PARAMS,
        cost_estimate=product_cost(pair, gate.shape[0]),
    )(gate, up, pair)


def other_input_terms(core, gate, up, pair, own, out):
    feature_count, token_count = own.shape
    shape = (out // 2, feature_count // out, token_count)
    return pl.pallas_call(
        other_input_kernel,
        out_shape=(jax.ShapeDtypeStruct(shape, F32), jax.ShapeDtypeStruct(shape, BF16)),
        in_specs=[IN_SMEM] + [IN_VMEM] * 4,
        out_specs=(IN_VMEM, IN_VMEM),
        scratch_shapes=[pltpu.VMEM((feature_count, token_count), F32)],
        compiler_params=PARAMS,
        cost_estimate=product_cost(pair, feature_count),
    )(core, gate, up, pair, own)


def split_kernel(index_ref, kept_ref, received_ref, mine_ref, *sent_refs):
    for k, ref in enumerate((mine_ref, *sent_refs)):
        at = index_ref[0] ^ k
        ref[...] = (kept_ref[at] + received_ref[at].astype(F32)).astype(ref.dtype)


def split_shares(index, kept, received):
    shape = kept.shape[1:]
    others = kept.shape[0] - 1
    return pl.pallas_call(
        split_kernel,
        out_shape=[jax.ShapeDtypeStruct(shape, F32)] + [jax.ShapeDtypeStruct(shape, BF16)] * others,
        in_specs=[IN_SMEM, IN_VMEM, IN_VMEM],
        out_specs=[IN_VMEM] * (others + 1),
        compiler_params=PARAMS,
        cost_estimate=pl.CostEstimate(
            flops=2 * kept.size, bytes_accessed=10 * kept.size, transcendentals=0
        ),
    )(index, kept, received)


def across_kernel(tokens_ref, out_ref):
    out_ref[...] = tokens_ref[...].astype(F32).T.astype(BF16)


def features_by_tokens(tokens):
    return pl.pallas_call(
        across_kernel,
        out_shape=jax.ShapeDtypeStruct(tokens.shape[::-1], BF16),
        compiler_params=PARAMS,
        cost_estimate=pl.CostEstimate(flops=0, bytes_accessed=4 * tokens.size, transcendentals=0),
    )(tokens)


def weight_kernel(factor, tokens_ref, own_ref, other_ref, out_ref, total_ref):
    step = pl.program_id(0)
    terms = []
    for block_ref in (own_ref, other_ref):
        terms.append(
            sum(
                lax.dot_general(
                    tokens_ref[k], block_ref[k], ROWS_BY_COLS, preferred_element_type=F32
                )
                for k in range(tokens_ref.shape[0])
            )
        )

    @pl.when(step == 0)
    def _():
        for side, term in enumerate(terms):
            total_ref[side] = term

    @pl.when(step > 0)
    def _():
        for side, term in enumerate(terms):
            total_ref[side] += term

    @pl.when(step == pl.num_programs(0) - 1)
    def _():
        width = total_ref.shape[2]
        for side in range(2):
            out_ref[:, side * width : (side + 1) * width] = (total_ref[side] * factor).astype(BF16)


def weight_terms(tokens, own, other, factor):
    dep, feature_count, token_count = tokens.shape
    width = own.shape[2]
    steps = 4
    block = pl.BlockSpec((dep // steps, token_count, width), lambda d: (d, 0, 0))
    return pl.pallas_call(
        functools.partial(weight_kernel, factor),
        out_shape=jax.ShapeDtypeStruct((feature_count, 2 * width), BF16),
        grid=(steps,),
        in_specs=[
            pl.BlockSpec((dep // steps, feature_count, token_count), lambda d: (d, 0, 0)),
            block,
            block,
        ],
        out_specs=pl.BlockSpec((feature_count, 2 * width), lambda d: (0, 0)),
        scratch_shapes=[pltpu.VMEM((2, feature_count, width), F32)],
        compiler_params=WHOLE,
        cost_estimate=pl.CostEstimate(
            flops=4 * dep * token_count * feature_count * width,
            bytes_accessed=2 * dep * token_count * (feature_count + 2 * width),
            transcendentals=0,
        ),
    )(tokens, own, other)


def finish_kernel(skips, side_ref, swapped_ref, gate_ref, up_ref):
    width = swapped_ref.shape[2] // 2
    half = gate_ref.shape[1] // 2
    blocks = len(skips)
    for u, out_ref in enumerate((gate_ref, up_ref)):
        for s in range(2):
            first = (side_ref[0] if s == 0 else 1 - side_ref[0]) * half
            for b, skip in enumerate(skips):
                at = pl.multiple_of(first + b * width, LANES)
                out_ref[:, pl.ds(at, width - skip)] = swapped_ref[u * blocks + b][
                    :, s * width + skip : (s + 1) * width
                ]


def finished(side, swapped, half, skips):
    shape = jax.ShapeDtypeStruct((swapped.shape[1], 2 * half), BF16)
    return pl.pallas_call(
        functools.partial(finish_kernel, skips),
        out_shape=(shape, shape),
        in_specs=[IN_SMEM, IN_VMEM],
        out_specs=(IN_VMEM, IN_VMEM),
        compiler_params=PARAMS,
        cost_estimate=pl.CostEstimate(
            flops=0, bytes_accessed=4 * swapped.size, transcendentals=0
        ),
    )(side, swapped)


def shards(tokens, grad_hidden, w_gate, w_up):
    token_count, feature_count = tokens.shape
    hidden = w_gate.shape[1]
    inp, out, dep = (lax.axis_size(name) for name in ("inp", "out", "dep"))
    factor = 1.0 / math.sqrt(token_count * dep)
    half = hidden // 2
    group = inp // 2
    rows = token_count // group
    pairs = [(i, i ^ 1) for i in range(inp)]
    alike = [[p + 2 * i for i in range(group)] for p in range(2)]
    place = lax.axis_index("inp")
    parity = place % 2
    own_side = parity.reshape(1)
    other_side = 1 - own_side

    given = partial_values(other_side, tokens, w_gate, w_up)
    own_side, given = lax.optimization_barrier((own_side, given))
    kept = partial_values(own_side, tokens, w_gate, w_up)
    kept = kept.astype(F32) + lax.ppermute(given, "inp", pairs).astype(F32)
    kept, w_gate, w_up, tokens = lax.optimization_barrier(
        (kept.astype(BF16), w_gate, w_up, tokens)
    )
    across = lax.all_gather(features_by_tokens(tokens), "dep", axis=0)
    terms = lax.all_to_all(
        kept.reshape(group, rows, hidden), "inp", 0, 0, axis_index_groups=alike
    )
    cotangent = lax.dynamic_slice(
        grad_hidden, ((place // 2) * rows, parity * half), (rows, half)
    )
    own_weights, other_weights = (
        [lax.dynamic_slice(w, (0, side * half), (feature_count, half)) for w in (w_gate, w_up)]
        for side in (parity, 1 - parity)
    )
    terms, own_weights, other_weights = lax.optimization_barrier(
        (terms, own_weights, other_weights)
    )
    own = lax.all_gather(
        grad_pair(terms, cotangent), "inp", axis=0, tiled=True, axis_index_groups=alike
    )
    other = lax.ppermute(own, "inp", pairs)

    width = 2 * LANES
    blocks = dep // 2
    starts = [min(b * width, half - width) for b in range(blocks)]
    skips = [b * width - s for b, s in enumerate(starts)]
    own_block = lax.all_to_all(dep_pieces(own, starts, width), "dep", 0, 0)
    own_share = own_input_terms(*own_weights, own)
    own_block, own_share = lax.optimization_barrier((own_block, own_share))
    other_block = lax.ppermute(own_block, "inp", pairs)

    at_out = lax.axis_index("out")
    core = (at_out % 2).reshape(1)
    chip = (at_out // 2).reshape(1)
    kept, given = other_input_terms(core, *other_weights, other, own_share, out)
    received = lax.ppermute(given, "out", [(i, i ^ 1) for i in range(out)])
    mine, *sent = split_shares(chip, kept, received)
    other_block, mine, sent = lax.optimization_barrier((other_block, mine, sent))
    for k, block in enumerate(sent, 1):
        mine = mine + lax.ppermute(block, "out", [(i, i ^ 2 * k) for i in range(out)]).astype(F32)
    grad_input = mine.astype(BF16).T

    grad = weight_terms(across, own_block, other_block, factor)
    swapped = lax.all_to_all(grad.reshape(dep, feature_count // dep, 2 * width), "dep", 0, 0)
    gate_grad, up_grad = finished(own_side, swapped, half, skips)
    return grad_input, gate_grad, up_grad


def solution(mesh):
    return jax.shard_map(
        shards,
        mesh=mesh,
        in_specs=(P("dep", "inp"), P("dep", "out"), P("inp", "out"), P("inp", "out")),
        out_specs=(P("dep", ("inp", "out")), P(("inp", "dep"), "out"), P(("inp", "dep"), "out")),
        check_vma=False,
    )
```

```python
import functools
import math

import jax
import jax.numpy as jnp
from jax import lax
from jax.experimental import pallas as pl
from jax.experimental.pallas import tpu as pltpu
from jax.sharding import PartitionSpec as P

BF16 = jnp.bfloat16
F32 = jnp.float32
LANES = 128
ROWS_BY_COLS = (((1,), (0,)), ((), ()))
COLS_BY_COLS = (((1,), (1,)), ((), ()))


def values_kernel(
    side_ref, tokens_hbm, gate_hbm, up_hbm, out_hbm, tokens_ref, gate_ref, up_ref, out_ref, sems
):
    half = gate_ref.shape[1]
    columns = pl.ds(pl.multiple_of(side_ref[0] * half, LANES), half)
    fetches = [
        pltpu.make_async_copy(tokens_hbm, tokens_ref, sems.at[0]),
        pltpu.make_async_copy(gate_hbm.at[:, columns], gate_ref, sems.at[1]),
        pltpu.make_async_copy(up_hbm.at[:, columns], up_ref, sems.at[2]),
    ]
    for fetch in fetches:
        fetch.start()
    fetches[0].wait()
    stores = []
    for u, w_ref in enumerate((gate_ref, up_ref)):
        fetches[1 + u].wait()
        part = lax.dot_general(
            tokens_ref[...], w_ref[...], ROWS_BY_COLS, preferred_element_type=F32
        )
        out_ref[u] = part.astype(out_ref.dtype)
        store = pltpu.make_async_copy(
            out_ref.at[u], out_hbm.at[:, pl.ds(u * half, half)], sems.at[3 + u]
        )
        store.start()
        stores.append(store)
    for store in stores:
        store.wait()


IN_HBM = pl.BlockSpec(memory_space=pltpu.HBM)
IN_SMEM = pl.BlockSpec(memory_space=pltpu.SMEM)
IN_VMEM = pl.BlockSpec(memory_space=pltpu.VMEM)
PARAMS = pltpu.CompilerParams(vmem_limit_bytes=16 * 2**20)
WHOLE = pltpu.CompilerParams(vmem_limit_bytes=60 * 2**20)
ROOM = pltpu.CompilerParams(vmem_limit_bytes=40 * 2**20)


def partial_values(side, tokens, w_gate, w_up, params):
    token_count, feature_count = tokens.shape
    half = w_gate.shape[1] // 2
    return pl.pallas_call(
        values_kernel,
        out_shape=jax.ShapeDtypeStruct((token_count, 2 * half), BF16),
        in_specs=[IN_SMEM, IN_HBM, IN_HBM, IN_HBM],
        out_specs=IN_HBM,
        scratch_shapes=[
            pltpu.VMEM((token_count, feature_count), BF16),
            pltpu.VMEM((feature_count, half), BF16),
            pltpu.VMEM((feature_count, half), BF16),
            pltpu.VMEM((2, token_count, half), BF16),
            pltpu.SemaphoreType.DMA((5,)),
        ],
        compiler_params=params,
        cost_estimate=pl.CostEstimate(
            flops=4 * token_count * feature_count * half,
            bytes_accessed=4 * feature_count * half + 4 * token_count * half,
            transcendentals=0,
        ),
    )(side, tokens, w_gate, w_up)


def grads_kernel(terms_ref, cotangent_ref, pair_ref):
    half = cotangent_ref.shape[1]
    values = terms_ref[0].astype(F32)
    for k in range(1, terms_ref.shape[0]):
        values = values + terms_ref[k].astype(F32)
    gate_value = values[:, :half]
    up_value = values[:, half:]
    cotangent = cotangent_ref[...].astype(F32)
    sigmoid_gate = jax.nn.sigmoid(gate_value)
    grad_gate = cotangent * up_value * sigmoid_gate * (1.0 + gate_value * (1.0 - sigmoid_gate))
    grad_upper = cotangent * gate_value * sigmoid_gate
    pair_ref[:, :half] = grad_gate.astype(BF16)
    pair_ref[:, half:] = grad_upper.astype(BF16)


def grad_pair(terms, cotangent):
    rows, half = cotangent.shape
    return pl.pallas_call(
        grads_kernel,
        out_shape=jax.ShapeDtypeStruct((rows, 2 * half), BF16),
        compiler_params=PARAMS,
        cost_estimate=pl.CostEstimate(
            flops=40 * rows * half,
            bytes_accessed=2 * terms.size + 8 * rows * half,
            transcendentals=rows * half,
        ),
    )(terms, cotangent)


def pieces_kernel(starts, pair_ref, pieces_ref):
    half = pair_ref.shape[1] // 2
    width = pieces_ref.shape[2]
    for u in range(2):
        for b, start in enumerate(starts):
            first = u * half + start
            pieces_ref[u * len(starts) + b] = pair_ref[:, first : first + width]


def dep_pieces(pair, starts, width):
    shape = (2 * len(starts), pair.shape[0], width)
    return pl.pallas_call(
        functools.partial(pieces_kernel, starts),
        out_shape=jax.ShapeDtypeStruct(shape, BF16),
        compiler_params=pltpu.CompilerParams(vmem_limit_bytes=40 * 2**20),
        cost_estimate=pl.CostEstimate(
            flops=0, bytes_accessed=4 * math.prod(shape), transcendentals=0
        ),
    )(pair)


def own_input_kernel(gate_ref, up_ref, pair_ref, out_ref):
    half = gate_ref.shape[1]
    out_ref[...] = sum(
        lax.dot_general(
            w_ref[...],
            pair_ref[:, u * half : (u + 1) * half],
            COLS_BY_COLS,
            preferred_element_type=F32,
        )
        for u, w_ref in enumerate((gate_ref, up_ref))
    )


def other_input_kernel(gate_ref, up_ref, pair_ref, own_ref, out_ref):
    half = gate_ref.shape[1]
    total = own_ref[...]
    for u, w_ref in enumerate((gate_ref, up_ref)):
        total = total + lax.dot_general(
            w_ref[...],
            pair_ref[:, u * half : (u + 1) * half],
            COLS_BY_COLS,
            preferred_element_type=F32,
        )
    out_ref[...] = total.astype(BF16)


def product_cost(pair, feature_count):
    return pl.CostEstimate(
        flops=2 * pair.size * feature_count,
        bytes_accessed=2 * pair.shape[1] * feature_count + 8 * pair.shape[0] * feature_count,
        transcendentals=0,
    )


def own_input_terms(gate, up, pair):
    return pl.pallas_call(
        own_input_kernel,
        out_shape=jax.ShapeDtypeStruct((gate.shape[0], pair.shape[0]), F32),
        compiler_params=PARAMS,
        cost_estimate=product_cost(pair, gate.shape[0]),
    )(gate, up, pair)


def other_input_terms(gate, up, pair, own):
    return pl.pallas_call(
        other_input_kernel,
        out_shape=jax.ShapeDtypeStruct(own.shape, BF16),
        compiler_params=PARAMS,
        cost_estimate=product_cost(pair, own.shape[0]),
    )(gate, up, pair, own)


def across_kernel(tokens_ref, out_ref):
    out_ref[...] = tokens_ref[...].astype(F32).T.astype(BF16)


def features_by_tokens(tokens):
    return pl.pallas_call(
        across_kernel,
        out_shape=jax.ShapeDtypeStruct(tokens.shape[::-1], BF16),
        compiler_params=PARAMS,
        cost_estimate=pl.CostEstimate(flops=0, bytes_accessed=4 * tokens.size, transcendentals=0),
    )(tokens)


def weight_kernel(factor, tokens_ref, own_ref, other_ref, out_ref, total_ref):
    step = pl.program_id(0)
    terms = []
    for block_ref in (own_ref, other_ref):
        terms.append(
            sum(
                lax.dot_general(
                    tokens_ref[k], block_ref[k], ROWS_BY_COLS, preferred_element_type=F32
                )
                for k in range(tokens_ref.shape[0])
            )
        )

    @pl.when(step == 0)
    def _():
        for side, term in enumerate(terms):
            total_ref[side] = term

    @pl.when(step > 0)
    def _():
        for side, term in enumerate(terms):
            total_ref[side] += term

    @pl.when(step == pl.num_programs(0) - 1)
    def _():
        width = total_ref.shape[2]
        for side in range(2):
            out_ref[:, side * width : (side + 1) * width] = (total_ref[side] * factor).astype(BF16)


def weight_terms(tokens, own, other, factor):
    dep, feature_count, token_count = tokens.shape
    width = own.shape[2]
    steps = 4
    block = pl.BlockSpec((dep // steps, token_count, width), lambda d: (d, 0, 0))
    return pl.pallas_call(
        functools.partial(weight_kernel, factor),
        out_shape=jax.ShapeDtypeStruct((feature_count, 2 * width), BF16),
        grid=(steps,),
        in_specs=[
            pl.BlockSpec((dep // steps, feature_count, token_count), lambda d: (d, 0, 0)),
            block,
            block,
        ],
        out_specs=pl.BlockSpec((feature_count, 2 * width), lambda d: (0, 0)),
        scratch_shapes=[pltpu.VMEM((2, feature_count, width), F32)],
        compiler_params=WHOLE,
        cost_estimate=pl.CostEstimate(
            flops=4 * dep * token_count * feature_count * width,
            bytes_accessed=2 * dep * token_count * (feature_count + 2 * width),
            transcendentals=0,
        ),
    )(tokens, own, other)


def finish_kernel(skips, side_ref, swapped_ref, gate_ref, up_ref):
    width = swapped_ref.shape[2] // 2
    half = gate_ref.shape[1] // 2
    blocks = len(skips)
    for u, out_ref in enumerate((gate_ref, up_ref)):
        for s in range(2):
            first = (side_ref[0] if s == 0 else 1 - side_ref[0]) * half
            for b, skip in enumerate(skips):
                at = pl.multiple_of(first + b * width, LANES)
                out_ref[:, pl.ds(at, width - skip)] = swapped_ref[u * blocks + b][
                    :, s * width + skip : (s + 1) * width
                ]


def finished(side, swapped, half, skips):
    shape = jax.ShapeDtypeStruct((swapped.shape[1], 2 * half), BF16)
    return pl.pallas_call(
        functools.partial(finish_kernel, skips),
        out_shape=(shape, shape),
        in_specs=[IN_SMEM, IN_VMEM],
        out_specs=(IN_VMEM, IN_VMEM),
        compiler_params=PARAMS,
        cost_estimate=pl.CostEstimate(
            flops=0, bytes_accessed=4 * swapped.size, transcendentals=0
        ),
    )(side, swapped)


def shards(tokens, grad_hidden, w_gate, w_up):
    token_count, feature_count = tokens.shape
    hidden = w_gate.shape[1]
    inp, out, dep = (lax.axis_size(name) for name in ("inp", "out", "dep"))
    factor = 1.0 / math.sqrt(token_count * dep)
    half = hidden // 2
    group = inp // 2
    rows = token_count // group
    pairs = [(i, i ^ 1) for i in range(inp)]
    alike = [[p + 2 * i for i in range(group)] for p in range(2)]
    place = lax.axis_index("inp")
    parity = place % 2
    own_side = parity.reshape(1)
    other_side = 1 - own_side

    given = partial_values(other_side, tokens, w_gate, w_up, WHOLE)
    own_side, given = lax.optimization_barrier((own_side, given))
    kept = partial_values(own_side, tokens, w_gate, w_up, ROOM)
    kept = kept.astype(F32) + lax.ppermute(given, "inp", pairs).astype(F32)
    kept, w_gate, w_up, tokens = lax.optimization_barrier(
        (kept.astype(BF16), w_gate, w_up, tokens)
    )
    across = lax.all_gather(features_by_tokens(tokens), "dep", axis=0)
    terms = lax.all_to_all(
        kept.reshape(group, rows, hidden), "inp", 0, 0, axis_index_groups=alike
    )
    cotangent = lax.dynamic_slice(
        grad_hidden, ((place // 2) * rows, parity * half), (rows, half)
    )
    own_weights, other_weights = (
        [lax.dynamic_slice(w, (0, side * half), (feature_count, half)) for w in (w_gate, w_up)]
        for side in (parity, 1 - parity)
    )
    terms, own_weights, other_weights = lax.optimization_barrier(
        (terms, own_weights, other_weights)
    )
    own = lax.all_gather(
        grad_pair(terms, cotangent), "inp", axis=0, tiled=True, axis_index_groups=alike
    )
    other = lax.ppermute(own, "inp", pairs)

    width = 2 * LANES
    blocks = dep // 2
    starts = [min(b * width, half - width) for b in range(blocks)]
    skips = [b * width - s for b, s in enumerate(starts)]
    own_block = lax.all_to_all(dep_pieces(own, starts, width), "dep", 0, 0)
    own_share = own_input_terms(*own_weights, own)
    own_block, own_share = lax.optimization_barrier((own_block, own_share))
    other_block = lax.ppermute(own_block, "inp", pairs)

    shares = other_input_terms(*other_weights, other, own_share)
    shares = lax.all_to_all(
        shares.reshape(out, feature_count // out, token_count), "out", 0, 0
    )
    grad_input = jnp.sum(shares.astype(F32), axis=0).astype(BF16).T

    grad = weight_terms(across, own_block, other_block, factor)
    swapped = lax.all_to_all(grad.reshape(dep, feature_count // dep, 2 * width), "dep", 0, 0)
    gate_grad, up_grad = finished(own_side, swapped, half, skips)
    return grad_input, gate_grad, up_grad


def solution(mesh):
    return jax.shard_map(
        shards,
        mesh=mesh,
        in_specs=(P("dep", "inp"), P("dep", "out"), P("inp", "out"), P("inp", "out")),
        out_specs=(P("dep", ("inp", "out")), P(("inp", "dep"), "out"), P(("inp", "dep"), "out")),
        check_vma=False,
    )
```
